32 devices in a mesh: grp: 2 (over x), path: 8 (over z, y), state: 2 (over core).
Axes of the slice: x: 2, y: 2, z: 4, core: 2. Of those that a mesh axis runs over, the one named last changes fastest.
Arguments:
- start_states: bfloat16 [2, 2, 128, 128, 128], P(None, 'state', 'path'), may hold values from -6 to 6
- block_gates: bfloat16 [3, 2, 128, 128], replicated, may hold values from -0.5 to 0.5
- cut_ops: float32 [2, 6, 2, 2, 2], replicated, may hold values from -4 to 4
- path_bits: int32 [16, 6], P(('grp', 'path')), parts along dimension 0, may hold values from 0 to 1
- left_pick: int32 [8], replicated, may hold values from 0 to 4194303
- right_pick: int32 [8], replicated, may hold values from 0 to 4194303
Outputs:
- amp_left: float32 [16, 2, 128, 128, 128], P('grp', 'state', 'path'), parts along dimension 0
- amp_right: float32 [16, 2, 128, 128, 128], P('grp', 'state', 'path'), parts along dimension 0
The draws below stay inside these ranges and needn't reach their ends.
There are 2 independent parts, one for each index of `grp`. The reference program is written for one: setup_inputs(seed, part) draws one part's arguments, and reference() takes and returns one part's arrays. A program takes and returns all parts, laid end to end along the dimension named above; an argument that names none is the same for every part. Nothing has to cross between parts.
All inputs are finite; a program needn't handle non-finite values.
Results may differ from the reference program's by a relative error of at most 0.0085.
Values may be sent and summed in bfloat16 or wider, within the bound.
A program may use at most 128 MiB of HBM per device.

```python
import math
import jax
import jax.numpy as jnp
from jax import lax

GATE_DIM = 128
BLOCKS = 3
CUT_BLOCK = 3
SEL = 8
CUTS = 6
PATHS = 8
N_STATE = 2


def plant(entries, own_key, smallest, top_value):
    longest = entries.shape.index(max(entries.shape))
    spots = []
    for shift in (0, 1):
        where = [jax.random.randint(jax.random.fold_in(own_key, axis), (), 0, length) for axis, length in enumerate(entries.shape)]
        where[longest] = (where[longest] + shift) % entries.shape[longest]
        spots.append(tuple(where))
    return entries.at[spots[0]].set(smallest).at[spots[1]].set(top_value)


def shard_levels(stream_key, extent, shards, low, top_value):
    def one(dim, parts):
        steps = jax.random.uniform(jax.random.fold_in(jax.random.fold_in(stream_key, 6), dim), (parts,), jnp.float32, low / len(shards), top_value / len(shards))
        return jnp.repeat(jnp.exp(steps), extent[dim] // parts).reshape((-1,) + (1,) * (len(extent) - dim - 1))

    factor_of = one(*shards[0])
    for cut in shards[1:]:
        factor_of = factor_of * one(*cut)
    return factor_of


def scatter_about(stream_key, dims, scale, most, split=(), kind=jnp.bfloat16):
    loudness = shard_levels(stream_key, dims, split, -0.22, 0.18) if split else 1.0
    array = jax.random.normal(stream_key, dims, jnp.float32) * scale * loudness
    return jnp.minimum(jnp.maximum(array, -most), most).astype(kind)


def setup_inputs(seed: int = 0, part: int = 0) -> dict:
    splits = jax.random.split(jax.random.key(seed), 7)
    part_splits = jax.random.split(jax.random.fold_in(splits[6], part), 7)
    return {
        "start_states": scatter_about(splits[0], (2, N_STATE, GATE_DIM, GATE_DIM, GATE_DIM), 1.0, 6.0, ((1, 2), (2, 8))),
        "block_gates": scatter_about(splits[1], (BLOCKS, 2, GATE_DIM, GATE_DIM), GATE_DIM ** -0.5, 0.5),
        "cut_ops": scatter_about(splits[2], (2, CUTS, 2, 2, 2), 2 ** -0.5, 4.0, (), jnp.float32),
        "path_bits": plant(jax.random.randint(part_splits[3], (PATHS, CUTS), 0, 2), jax.random.fold_in(part_splits[3], 1), 0, 1).astype(jnp.int32),
        "left_pick": plant(jax.random.randint(splits[4], (SEL,), 0, N_STATE * GATE_DIM ** 3), jax.random.fold_in(splits[4], 1), 0, (N_STATE * GATE_DIM ** 3) - 1).astype(jnp.int32),
        "right_pick": plant(jax.random.randint(splits[5], (SEL,), 0, N_STATE * GATE_DIM ** 3), jax.random.fold_in(splits[5], 1), 0, (N_STATE * GATE_DIM ** 3) - 1).astype(jnp.int32),
    }


def kron_cut(cut_pair, bit_row):
    result = jnp.eye(GATE_DIM // 2 ** CUT_BLOCK, dtype=jnp.float32)
    for position in reversed(range(CUT_BLOCK)):
        picked = jnp.where(bit_row[position] == 1, cut_pair[position, 1], cut_pair[position, 0])
        result = jnp.kron(result, picked)
    return result

def mixed_gate(matrix, cut_pair, bit_row):
    product = jnp.dot(matrix.astype(jnp.float32), kron_cut(cut_pair, bit_row), precision=lax.Precision.HIGHEST)
    return product.astype(jnp.bfloat16)

def apply_last(matrix, states):
    return jnp.einsum('...j,ij->...i', states.astype(jnp.float32), matrix.astype(jnp.float32)).astype(jnp.bfloat16)

def apply_middle(matrix, states):
    return jnp.einsum('txjz,ij->txiz', states.astype(jnp.float32), matrix.astype(jnp.float32)).astype(jnp.bfloat16)

def apply_top(matrix, states):
    viewed = states.reshape(GATE_DIM, 2, GATE_DIM, GATE_DIM)
    turned = jnp.einsum('iw,wuyz->iuyz', matrix.astype(jnp.float32), viewed.astype(jnp.float32))
    return turned.astype(jnp.bfloat16).reshape(N_STATE, GATE_DIM, GATE_DIM, GATE_DIM)

def reference(start_states, block_gates, cut_ops, path_bits, left_pick, right_pick):
    base_state = jnp.stack([apply_last(block_gates[0, which_half], start_states[which_half]) for which_half in range(2)])
    powers = 2 ** jnp.arange(CUT_BLOCK, dtype=jnp.int32)

    def first_variant(variant_code):
        bit_row = variant_code // powers % 2
        return jnp.stack([apply_middle(mixed_gate(block_gates[1, which_half], cut_ops[which_half, :CUT_BLOCK], bit_row), base_state[which_half]) for which_half in range(2)])
    variants = lax.map(first_variant, jnp.arange(2 ** CUT_BLOCK, dtype=jnp.int32))

    def one_path(bit_row):
        variant_code = jnp.sum(bit_row[:CUT_BLOCK] * powers).astype(jnp.int32)
        first_state = lax.dynamic_index_in_dim(variants, variant_code, 0, keepdims=False)
        finals = jnp.stack([apply_top(mixed_gate(block_gates[2, which_half], cut_ops[which_half, CUT_BLOCK:], bit_row[CUT_BLOCK:]), first_state[which_half]) for which_half in range(2)])
        left_vals = finals[0].reshape(-1)[left_pick]
        right_vals = finals[1].reshape(-1)[right_pick]
        return (finals, left_vals, right_vals)
    finals, left_vals, right_vals = lax.map(one_path, path_bits)
    norm_scale = 1.0 / math.sqrt(PATHS)
    left_flat = finals[:, 0].reshape(PATHS, -1)
    right_flat = finals[:, 1].reshape(PATHS, -1)
    amp_left = jnp.dot(right_vals.T, left_flat, preferred_element_type=jnp.float32) * norm_scale
    amp_right = jnp.dot(left_vals.T, right_flat, preferred_element_type=jnp.float32) * norm_scale
    out_shape = (SEL, N_STATE, GATE_DIM, GATE_DIM, GATE_DIM)
    return (amp_left.reshape(out_shape), amp_right.reshape(out_shape))
```

```python
import functools
import math

import jax
import jax.numpy as jnp
from jax import lax
from jax.experimental import pallas as pl
from jax.experimental.pallas import tpu as pltpu
from jax.sharding import PartitionSpec as P


def mixes(gates, cuts, bits):
    dimension = gates.shape[-1]
    count = bits.shape[1]
    rows = lax.broadcasted_iota(jnp.int32, (dimension, dimension), 0)
    cols = lax.broadcasted_iota(jnp.int32, (dimension, dimension), 1)
    block = 2**count
    kernel = jnp.where(rows // block == cols // block, 1.0, 0.0).astype(jnp.float32)
    for k in reversed(range(count)):
        picked = jnp.where(
            (bits[:, k] == 1)[:, None, None, None], cuts[None, :, k, 1], cuts[None, :, k, 0]
        )
        low_row = rows // 2**k % 2 == 1
        low_col = cols // 2**k % 2 == 1
        entry = [[picked[:, :, a, b, None, None] for b in range(2)] for a in range(2)]
        factor = jnp.where(
            low_row,
            jnp.where(low_col, entry[1][1], entry[1][0]),
            jnp.where(low_col, entry[0][1], entry[0][0]),
        )
        kernel = kernel * factor
    return jnp.einsum(
        "hij,phjk->phik",
        gates.astype(jnp.float32),
        kernel,
        precision=lax.Precision.HIGHEST,
        preferred_element_type=jnp.float32,
    ).astype(jnp.bfloat16)


def turn_kernel(paths, half_block, states_ref, top_ref, middle_ref, out_ref, turned_ref):
    dimension = middle_ref.shape[-1]
    rows = top_ref.shape[0]

    def mix_top(y, carry):
        block = states_ref[:, 0, y].reshape(dimension, dimension)
        turned_ref[pl.ds(y, rows, stride=dimension), :] = jnp.dot(
            top_ref[...], block, preferred_element_type=jnp.float32
        )
        return carry

    lax.fori_loop(0, dimension, mix_top, 0, unroll=4)

    def mix_middle(p, carry):
        matrix = middle_ref[p]
        for side in range(2):
            for w in range(half_block):
                row = (side * paths + p) * half_block + w
                start = pl.multiple_of(row * dimension, dimension)
                block = turned_ref[pl.ds(start, dimension), :].astype(jnp.bfloat16)
                out_ref[side, p, w] = jnp.dot(
                    matrix, block, preferred_element_type=jnp.float32
                ).astype(jnp.bfloat16)
        return carry

    lax.fori_loop(0, paths, mix_middle, 0)


def turn(states, top, middle, u):
    owners, _, dimension, near, _ = states.shape
    paths = middle.shape[0]
    half_block = near // 2
    return pl.pallas_call(
        functools.partial(turn_kernel, paths, half_block),
        grid=(1,),
        in_specs=[
            pl.BlockSpec(
                (owners, 1, dimension, near, dimension),
                lambda i: (0, u, 0, 0, 0),
                pipeline_mode=pl.Buffered(1),
            ),
            pl.BlockSpec(top.shape, lambda i: (0, 0)),
            pl.BlockSpec(middle.shape, lambda i: (0, 0, 0)),
        ],
        out_specs=pl.BlockSpec(
            (2, paths, half_block, dimension, dimension), lambda i: (0, 0, 0, 0, 0)
        ),
        out_shape=jax.ShapeDtypeStruct(
            (2, paths, half_block, dimension, dimension), jnp.bfloat16
        ),
        scratch_shapes=[pltpu.VMEM((top.shape[0] * dimension, dimension), jnp.float32)],
        compiler_params=pltpu.CompilerParams(vmem_limit_bytes=50 * 2**20),
        cost_estimate=pl.CostEstimate(
            flops=4 * top.shape[0] * dimension**3,
            bytes_accessed=4 * dimension**3 * 2,
            transcendentals=0,
        ),
    )(states, top, middle)


def join_kernel(paths, selected, vals_ref, *refs):
    mine = refs[:2]
    other = refs[2:4]
    outs = refs[4:]
    c = vals_ref[2 * paths * selected]
    dimension = mine[0].shape[-1]
    step = 32

    for u in range(2):
        for source, which in ((mine[u], 0), (other[u], 1)):
            half = c if which == 0 else 1.0 - c
            for h in range(2):

                @pl.when(half == float(h))
                def _(source=source, h=h, u=u):
                    def chunk(i, carry):
                        start = pl.multiple_of(i * step, step)
                        loaded = [
                            source[p, 0, pl.ds(start, step), :].astype(jnp.float32)
                            for p in range(paths)
                        ]
                        for j in range(selected):
                            base = (1 - h) * paths * selected + j
                            total = loaded[0] * vals_ref[base]
                            for p in range(1, paths):
                                total = total + loaded[p] * vals_ref[base + p * selected]
                            outs[h][j, 0, u, pl.ds(start, step), :] = total
                        return carry

                    lax.fori_loop(0, dimension // step, chunk, 0)


def join(vals, mine, other):
    paths, half_block, dimension, _ = mine[0].shape
    selected = vals.shape[0] // (2 * paths)
    spec = pl.BlockSpec((paths, 1, dimension, dimension), lambda w, *_: (0, w, 0, 0))
    out_spec = pl.BlockSpec(
        (selected, 1, 2, dimension, dimension), lambda w, *_: (0, w, 0, 0, 0)
    )
    out = jax.ShapeDtypeStruct((selected, half_block, 2, dimension, dimension), jnp.float32)
    return pl.pallas_call(
        functools.partial(join_kernel, paths, selected),
        grid_spec=pltpu.PrefetchScalarGridSpec(
            num_scalar_prefetch=1,
            grid=(half_block,),
            in_specs=[spec] * 4,
            out_specs=[out_spec] * 2,
        ),
        out_shape=[out, out],
        compiler_params=pltpu.CompilerParams(vmem_limit_bytes=50 * 2**20),
    )(vals, *mine, *other)


def body(start_states, block_gates, cut_ops, path_bits, left_pick, right_pick):
    sections = path_bits.shape[1] // 2
    c = lax.axis_index("state")
    k = lax.axis_index("path")
    owners = lax.axis_size("path")
    dimension = start_states.shape[-1]
    half_block = dimension // (2 * owners)
    near = 2 * half_block
    per_device = path_bits.shape[0]
    paths = owners * per_device
    selected = left_pick.shape[0]

    mine = lax.all_to_all(start_states, "state", split_axis=0, concat_axis=1, tiled=True)
    mine = mine.reshape(2, half_block, 2, dimension, dimension)
    laid = jnp.transpose(mine, (2, 3, 0, 1, 4)).reshape(2, dimension, near, dimension)
    gate = lax.dynamic_index_in_dim(block_gates[0], c, 0, keepdims=False)
    base = jnp.einsum(
        "uyvz,iz->uyvi", laid, gate, preferred_element_type=jnp.float32
    ).astype(jnp.bfloat16)

    picks = jnp.stack([left_pick, right_pick])
    own_picks = lax.dynamic_index_in_dim(picks, c, 0, keepdims=False)
    z_hot = (own_picks[:, None] % dimension == jnp.arange(dimension)[None, :]).astype(jnp.bfloat16)
    lanes = jnp.einsum("jz,uyvz->juyv", z_hot, base, preferred_element_type=jnp.float32)
    u_own = own_picks // (dimension * dimension) % 2
    near_pick = jnp.where(u_own[:, None, None] == 1, lanes[:, 1], lanes[:, 0])
    small = jnp.concatenate(
        [
            near_pick.astype(jnp.bfloat16).reshape(-1),
            jnp.pad(path_bits.astype(jnp.bfloat16), ((0, 0), (0, dimension - 2 * sections))).reshape(-1),
        ]
    )
    pooled = lax.all_gather(small, ("path", "state"), axis=0)
    size = selected * dimension * near
    bits = pooled[:, size:].reshape(owners, 2, per_device, dimension)[:, 0, :, : 2 * sections]
    bits = bits.reshape(paths, 2 * sections).astype(jnp.int32)
    columns = pooled[:, :size].reshape(owners, 2, selected, dimension, near)

    gathered = lax.all_gather(base, "path", axis=0)

    mix1 = mixes(block_gates[1], cut_ops[:, :sections], bits[:, :sections])
    mix2 = mixes(block_gates[2], cut_ops[:, sections:], bits[:, sections:])
    turned2 = jnp.transpose(
        mix2.reshape(paths, 2, dimension, 2, owners, half_block), (0, 1, 2, 4, 3, 5)
    ).reshape(paths, 2, dimension, dimension)

    row_y = picks // dimension % dimension
    row_w = picks // (dimension * dimension) // 2
    y_hot = (row_y[:, :, None] == jnp.arange(dimension)).astype(jnp.bfloat16)
    w_hot = (row_w[:, :, None] == jnp.arange(dimension)).astype(jnp.bfloat16)
    m1_rows = jnp.einsum("hjy,phyk->phjk", y_hot, mix1, preferred_element_type=jnp.float32)
    m2_rows = jnp.einsum("hjw,phwv->phjv", w_hot, turned2, preferred_element_type=jnp.float32)
    cols = jnp.transpose(columns, (1, 2, 3, 0, 4)).reshape(2, selected, dimension, dimension)
    first = jnp.einsum(
        "phjy,hjyv->phjv",
        m1_rows.astype(jnp.bfloat16),
        cols,
        preferred_element_type=jnp.float32,
    ).astype(jnp.bfloat16)
    vals = jnp.sum(first.astype(jnp.float32) * m2_rows, axis=-1).astype(jnp.bfloat16)
    scale = 1.0 / math.sqrt(paths)
    flat = jnp.transpose(vals.astype(jnp.float32) * scale, (1, 0, 2)).reshape(-1)
    flat = jnp.concatenate([flat, c.astype(jnp.float32)[None]])

    own2 = lax.dynamic_index_in_dim(turned2, c, 1, keepdims=False)
    own2 = own2.reshape(paths, 2, owners, half_block, dimension)
    own2 = lax.dynamic_index_in_dim(own2, k, 2, keepdims=False)
    own2 = jnp.where(c == 1, own2[:, ::-1], own2)
    top = jnp.transpose(own2, (1, 0, 2, 3)).reshape(2 * paths * half_block, dimension)
    middle = lax.dynamic_index_in_dim(mix1, c, 1, keepdims=False)

    kept, arrived = [], []
    for u in range(2):
        both = turn(gathered, top, middle, u)
        kept.append(both[0])
        arrived.append(lax.ppermute(both[1], "state", [(0, 1), (1, 0)]))
    outs = join(flat, kept, arrived)
    return tuple(out.reshape(selected, 1, near, dimension, dimension) for out in outs)


def solution(mesh):
    in_specs = (P(None, "state", "path", None, None), P(), P(), P(("grp", "path"), None), P(), P())
    out_specs = (P("grp", "state", "path", None, None), P("grp", "state", "path", None, None))
    return jax.shard_map(body, mesh=mesh, in_specs=in_specs, out_specs=out_specs, check_vma=False)
```

```python
import functools
import math

import jax
import jax.numpy as jnp
from jax import lax
from jax.experimental import pallas as pl
from jax.experimental.pallas import tpu as pltpu
from jax.sharding import PartitionSpec as P


MESH = pl.DeviceIdType.MESH


def gather_kernel(n, pairs, base_ref, out_ref, own_sem, send_sem, recv_sem):
    g, k, c = lax.axis_index("grp"), lax.axis_index("path"), lax.axis_index("state")
    dimension = base_ref.shape[1]
    odd = lax.rem(k, 2)
    pos = (1 - odd) * (k // 2) + odd * (n - 1 - k // 2)

    def place(p):
        p = lax.rem(p + n, n)
        high = p // (n // 2)
        return (1 - high) * (2 * p) + high * (2 * (n - 1 - p) + 1)

    right, left = (g, place(pos + 1), c), (g, place(pos - 1), c)
    side = lax.rem(g, 2) if pairs else 0
    partner = (g + 1 - 2 * side, k, c)

    barrier = pltpu.get_barrier_semaphore()
    greeted = (right, left, partner) if pairs else (right, left)
    for other in greeted:
        pl.semaphore_signal(barrier, inc=1, device_id=other, device_id_type=MESH)
    pl.semaphore_wait(barrier, len(greeted))

    outer = (dimension + 2) // 3 if pairs else dimension // 2
    middle = dimension - 2 * outer if pairs else dimension - outer

    def cut(start, length):
        first = (length + 1) // 2
        return ((start, first), (start + first, length - first))

    far = dimension - outer
    runs = (
        cut(side * far if pairs else 0, outer),
        cut(outer, middle),
        cut((1 - side) * far if pairs else 0, outer),
    )

    own = pltpu.make_async_copy(base_ref, out_ref.at[k], own_sem)
    own.start()

    def copy(stream, u, step, piece, target):
        start, length = runs[stream][piece]
        hop = (step - 1, 1 - step, step)[stream]
        rows = pl.ds(start, length)
        block = place(pos - hop)
        source = base_ref.at[u, rows] if stream < 2 and step == 1 else out_ref.at[block, u, rows]
        return pltpu.make_async_remote_copy(
            src_ref=source,
            dst_ref=out_ref.at[block, u, rows],
            send_sem=send_sem.at[stream, u, step - 1, piece],
            recv_sem=recv_sem.at[stream, u, step - 1, piece],
            device_id=target,
            device_id_type=MESH,
        )

    def arriving(stream, u, step, piece):
        start, length = runs[stream][piece]
        hop = (step, -step, step)[stream]
        ref = out_ref.at[place(pos - hop), u, pl.ds(start, length)]
        return pltpu.make_async_remote_copy(
            src_ref=ref,
            dst_ref=ref,
            send_sem=send_sem.at[stream, u, step - 1, piece],
            recv_sem=recv_sem.at[stream, u, step - 1, piece],
            device_id=left,
            device_id_type=MESH,
        )

    started = []

    def start(item):
        item.start()
        started.append(item)

    def advance(u, step):
        for piece in range(2):
            for stream, target in ((0, right), (1, left)):
                if step > 0:
                    arriving(stream, u, step, piece).wait_recv()
                if step < n - 1:
                    start(copy(stream, u, step + 1, piece, target))
                if pairs and stream == 0 and step > 0:
                    start(passed(u, step, piece))

    def passed(u, step, piece):
        first, length = runs[0][piece]
        ref = out_ref.at[place(pos - step), u, pl.ds(first, length)]
        return pltpu.make_async_remote_copy(
            src_ref=ref,
            dst_ref=ref,
            send_sem=send_sem.at[2, u, step - 1, piece],
            recv_sem=recv_sem.at[2, u, step - 1, piece],
            device_id=partner,
            device_id_type=MESH,
        )

    for step in range(n - 1):
        advance(0, step)
    advance(1, 0)
    advance(0, n - 1)
    for step in range(1, n):
        advance(1, step)
    if pairs:
        for u in range(2):
            for step in range(1, n):
                for piece in range(2):
                    arriving(2, u, step, piece).wait_recv()
    for item in started:
        item.wait_send()
    own.wait()


def gather_rows(base, n):
    pairs = lax.axis_size("grp") % 2 == 0
    streams = 3 if pairs else 2
    return pl.pallas_call(
        functools.partial(gather_kernel, n, pairs),
        out_shape=jax.ShapeDtypeStruct((n,) + base.shape, base.dtype),
        in_specs=[pl.BlockSpec(memory_space=pltpu.VMEM)],
        out_specs=pl.BlockSpec(memory_space=pl.ANY),
        scratch_shapes=[
            pltpu.SemaphoreType.DMA,
            pltpu.SemaphoreType.DMA((streams, 2, n - 1, 2)),
            pltpu.SemaphoreType.DMA((streams, 2, n - 1, 2)),
        ],
        compiler_params=pltpu.CompilerParams(
            collective_id=0, has_side_effects=True, vmem_limit_bytes=8 * 2**20
        ),
    )(base)


def mixes(gates, cuts, bits):
    dimension = gates.shape[-1]
    count = bits.shape[1]
    rows = lax.broadcasted_iota(jnp.int32, (dimension, dimension), 0)
    cols = lax.broadcasted_iota(jnp.int32, (dimension, dimension), 1)
    block = 2**count
    kernel = jnp.where(rows // block == cols // block, 1.0, 0.0).astype(jnp.float32)
    for k in reversed(range(count)):
        picked = jnp.where(
            (bits[:, k] == 1)[:, None, None, None], cuts[None, :, k, 1], cuts[None, :, k, 0]
        )
        low_row = rows // 2**k % 2 == 1
        low_col = cols // 2**k % 2 == 1
        entry = [[picked[:, :, a, b, None, None] for b in range(2)] for a in range(2)]
        factor = jnp.where(
            low_row,
            jnp.where(low_col, entry[1][1], entry[1][0]),
            jnp.where(low_col, entry[0][1], entry[0][0]),
        )
        kernel = kernel * factor
    return jnp.einsum(
        "hij,phjk->phik",
        gates.astype(jnp.float32),
        kernel,
        precision=lax.Precision.HIGHEST,
        preferred_element_type=jnp.float32,
    ).astype(jnp.bfloat16)


def turn_kernel(paths, half_block, states_ref, top_ref, middle_ref, out_ref, turned_ref):
    dimension = middle_ref.shape[-1]
    rows = top_ref.shape[0]

    def mix_top(y, carry):
        block = states_ref[:, 0, y].reshape(dimension, dimension)
        turned_ref[pl.ds(y, rows, stride=dimension), :] = jnp.dot(
            top_ref[...], block, preferred_element_type=jnp.float32
        )
        return carry

    lax.fori_loop(0, dimension, mix_top, 0, unroll=4)

    def mix_middle(p, carry):
        matrix = middle_ref[p]
        for side in range(2):
            for w in range(half_block):
                row = (side * paths + p) * half_block + w
                start = pl.multiple_of(row * dimension, dimension)
                block = turned_ref[pl.ds(start, dimension), :].astype(jnp.bfloat16)
                out_ref[side, p, w] = jnp.dot(
                    matrix, block, preferred_element_type=jnp.float32
                ).astype(jnp.bfloat16)
        return carry

    lax.fori_loop(0, paths, mix_middle, 0)


def turn(states, top, middle, u):
    owners, _, dimension, near, _ = states.shape
    paths = middle.shape[0]
    half_block = near // 2
    return pl.pallas_call(
        functools.partial(turn_kernel, paths, half_block),
        grid=(1,),
        in_specs=[
            pl.BlockSpec(
                (owners, 1, dimension, near, dimension),
                lambda i: (0, u, 0, 0, 0),
                pipeline_mode=pl.Buffered(1),
            ),
            pl.BlockSpec(top.shape, lambda i: (0, 0)),
            pl.BlockSpec(middle.shape, lambda i: (0, 0, 0)),
        ],
        out_specs=pl.BlockSpec(
            (2, paths, half_block, dimension, dimension), lambda i: (0, 0, 0, 0, 0)
        ),
        out_shape=jax.ShapeDtypeStruct(
            (2, paths, half_block, dimension, dimension), jnp.bfloat16
        ),
        scratch_shapes=[pltpu.VMEM((top.shape[0] * dimension, dimension), jnp.float32)],
        compiler_params=pltpu.CompilerParams(vmem_limit_bytes=50 * 2**20),
        cost_estimate=pl.CostEstimate(
            flops=4 * top.shape[0] * dimension**3,
            bytes_accessed=4 * dimension**3 * 2,
            transcendentals=0,
        ),
    )(states, top, middle)


def join_kernel(paths, selected, vals_ref, *refs):
    mine = refs[:2]
    other = refs[2:4]
    outs = refs[4:]
    c = vals_ref[2 * paths * selected]
    dimension = mine[0].shape[-1]
    step = 32

    for u in range(2):
        for source, which in ((mine[u], 0), (other[u], 1)):
            half = c if which == 0 else 1.0 - c
            for h in range(2):

                @pl.when(half == float(h))
                def _(source=source, h=h, u=u):
                    def chunk(i, carry):
                        start = pl.multiple_of(i * step, step)
                        loaded = [
                            source[p, 0, pl.ds(start, step), :].astype(jnp.float32)
                            for p in range(paths)
                        ]
                        for j in range(selected):
                            base = (1 - h) * paths * selected + j
                            total = loaded[0] * vals_ref[base]
                            for p in range(1, paths):
                                total = total + loaded[p] * vals_ref[base + p * selected]
                            outs[h][j, 0, u, pl.ds(start, step), :] = total
                        return carry

                    lax.fori_loop(0, dimension // step, chunk, 0)


def join(vals, mine, other):
    paths, half_block, dimension, _ = mine[0].shape
    selected = vals.shape[0] // (2 * paths)
    spec = pl.BlockSpec((paths, 1, dimension, dimension), lambda w, *_: (0, w, 0, 0))
    out_spec = pl.BlockSpec(
        (selected, 1, 2, dimension, dimension), lambda w, *_: (0, w, 0, 0, 0)
    )
    out = jax.ShapeDtypeStruct((selected, half_block, 2, dimension, dimension), jnp.float32)
    return pl.pallas_call(
        functools.partial(join_kernel, paths, selected),
        grid_spec=pltpu.PrefetchScalarGridSpec(
            num_scalar_prefetch=1,
            grid=(half_block,),
            in_specs=[spec] * 4,
            out_specs=[out_spec] * 2,
        ),
        out_shape=[out, out],
        compiler_params=pltpu.CompilerParams(vmem_limit_bytes=50 * 2**20),
    )(vals, *mine, *other)


def body(start_states, block_gates, cut_ops, path_bits, left_pick, right_pick):
    sections = path_bits.shape[1] // 2
    c = lax.axis_index("state")
    k = lax.axis_index("path")
    owners = lax.axis_size("path")
    dimension = start_states.shape[-1]
    half_block = dimension // (2 * owners)
    near = 2 * half_block
    per_device = path_bits.shape[0]
    paths = owners * per_device
    selected = left_pick.shape[0]

    mine = lax.all_to_all(start_states, "state", split_axis=0, concat_axis=1, tiled=True)
    mine = mine.reshape(2, half_block, 2, dimension, dimension)
    laid = jnp.transpose(mine, (2, 3, 0, 1, 4)).reshape(2, dimension, near, dimension)
    gate = lax.dynamic_index_in_dim(block_gates[0], c, 0, keepdims=False)
    base = jnp.einsum(
        "uyvz,iz->uyvi", laid, gate, preferred_element_type=jnp.float32
    ).astype(jnp.bfloat16)

    picks = jnp.stack([left_pick, right_pick])
    own_picks = lax.dynamic_index_in_dim(picks, c, 0, keepdims=False)
    z_hot = (own_picks[:, None] % dimension == jnp.arange(dimension)[None, :]).astype(jnp.bfloat16)
    lanes = jnp.einsum("jz,uyvz->juyv", z_hot, base, preferred_element_type=jnp.float32)
    u_own = own_picks // (dimension * dimension) % 2
    near_pick = jnp.where(u_own[:, None, None] == 1, lanes[:, 1], lanes[:, 0])
    small = jnp.concatenate(
        [
            near_pick.astype(jnp.bfloat16).reshape(-1),
            jnp.pad(path_bits.astype(jnp.bfloat16), ((0, 0), (0, dimension - 2 * sections))).reshape(-1),
        ]
    )
    pooled = lax.all_gather(small, ("path", "state"), axis=0)
    size = selected * dimension * near
    bits = pooled[:, size:].reshape(owners, 2, per_device, dimension)[:, 0, :, : 2 * sections]
    bits = bits.reshape(paths, 2 * sections).astype(jnp.int32)
    columns = pooled[:, :size].reshape(owners, 2, selected, dimension, near)

    if owners % 2 == 0 and 4 <= owners <= 8:
        base, bits = lax.optimization_barrier((base, bits))
        gathered = gather_rows(base, owners)
    else:
        gathered = lax.all_gather(base, "path", axis=0)

    mix1 = mixes(block_gates[1], cut_ops[:, :sections], bits[:, :sections])
    mix2 = mixes(block_gates[2], cut_ops[:, sections:], bits[:, sections:])
    turned2 = jnp.transpose(
        mix2.reshape(paths, 2, dimension, 2, owners, half_block), (0, 1, 2, 4, 3, 5)
    ).reshape(paths, 2, dimension, dimension)

    row_y = picks // dimension % dimension
    row_w = picks // (dimension * dimension) // 2
    y_hot = (row_y[:, :, None] == jnp.arange(dimension)).astype(jnp.bfloat16)
    w_hot = (row_w[:, :, None] == jnp.arange(dimension)).astype(jnp.bfloat16)
    m1_rows = jnp.einsum("hjy,phyk->phjk", y_hot, mix1, preferred_element_type=jnp.float32)
    m2_rows = jnp.einsum("hjw,phwv->phjv", w_hot, turned2, preferred_element_type=jnp.float32)
    cols = jnp.transpose(columns, (1, 2, 3, 0, 4)).reshape(2, selected, dimension, dimension)
    first = jnp.einsum(
        "phjy,hjyv->phjv",
        m1_rows.astype(jnp.bfloat16),
        cols,
        preferred_element_type=jnp.float32,
    ).astype(jnp.bfloat16)
    vals = jnp.sum(first.astype(jnp.float32) * m2_rows, axis=-1).astype(jnp.bfloat16)
    scale = 1.0 / math.sqrt(paths)
    flat = jnp.transpose(vals.astype(jnp.float32) * scale, (1, 0, 2)).reshape(-1)
    flat = jnp.concatenate([flat, c.astype(jnp.float32)[None]])

    own2 = lax.dynamic_index_in_dim(turned2, c, 1, keepdims=False)
    own2 = own2.reshape(paths, 2, owners, half_block, dimension)
    own2 = lax.dynamic_index_in_dim(own2, k, 2, keepdims=False)
    own2 = jnp.where(c == 1, own2[:, ::-1], own2)
    top = jnp.transpose(own2, (1, 0, 2, 3)).reshape(2 * paths * half_block, dimension)
    middle = lax.dynamic_index_in_dim(mix1, c, 1, keepdims=False)

    kept, arrived = [], []
    for u in range(2):
        both = turn(gathered, top, middle, u)
        kept.append(both[0])
        arrived.append(lax.ppermute(both[1], "state", [(0, 1), (1, 0)]))
    outs = join(flat, kept, arrived)
    return tuple(out.reshape(selected, 1, near, dimension, dimension) for out in outs)


def solution(mesh):
    in_specs = (P(None, "state", "path", None, None), P(), P(), P(("grp", "path"), None), P(), P())
    out_specs = (P("grp", "state", "path", None, None), P("grp", "state", "path", None, None))
    return jax.shard_map(body, mesh=mesh, in_specs=in_specs, out_specs=out_specs, check_vma=False)
```

```python
import functools
import math

import jax
import jax.numpy as jnp
from jax import lax
from jax.experimental import pallas as pl
from jax.experimental.pallas import tpu as pltpu
from jax.sharding import PartitionSpec as P


MESH = pl.DeviceIdType.MESH


def window_kernel(
    n,
    pairs,
    scale,
    base_ref,
    ext_ref,
    first_ref,
    top_ref,
    first_pick_ref,
    top_pick_ref,
    kept_ref,
    arrived_ref,
    vals_ref,
    held_ref,
    exts_ref,
    middle_ref,
    stack_ref,
    turned_ref,
    final_ref,
    vals_buf,
    own_sem,
    send_sem,
    recv_sem,
    ext_send,
    ext_recv,
    vals_sem,
    kept_sem,
    swap_sem,
):
    g, k, c = lax.axis_index("grp"), lax.axis_index("path"), lax.axis_index("state")
    dimension = base_ref.shape[1]
    variants, selected = top_pick_ref.shape[:2]
    half_block = top_ref.shape[2]
    odd = lax.rem(k, 2)
    pos = (1 - odd) * (k // 2) + odd * (n - 1 - k // 2)

    def place(p):
        p = lax.rem(p + n, n)
        high = p // (n // 2)
        return (1 - high) * (2 * p) + high * (2 * (n - 1 - p) + 1)

    right, left = (g, place(pos + 1), c), (g, place(pos - 1), c)
    side = lax.rem(g, 2) if pairs else 0
    partner = (g + 1 - 2 * side, k, c)
    twin = (g, k, 1 - c)

    barrier = pltpu.get_barrier_semaphore()
    greeted = [(g, lax.rem(k + d, n), c) for d in range(1, n)] + [twin]
    if pairs:
        greeted.append(partner)
    for other in greeted:
        pl.semaphore_signal(barrier, inc=1, device_id=other, device_id_type=MESH)
    pl.semaphore_wait(barrier, len(greeted))

    outer = (dimension + 2) // 3 if pairs else dimension // 2
    middle = dimension - 2 * outer if pairs else dimension - outer

    def cut(start, length):
        half = (length + 1) // 2
        return ((start, half), (start + half, length - half))

    far = dimension - outer
    runs = (
        cut(side * far if pairs else 0, outer),
        cut(outer, middle),
        cut((1 - side) * far if pairs else 0, outer),
    )

    started = []

    def start(item):
        item.start()
        started.append(item)

    def remote(source, target_ref, send, recv, device):
        return pltpu.make_async_remote_copy(
            src_ref=source,
            dst_ref=target_ref,
            send_sem=send,
            recv_sem=recv,
            device_id=device,
            device_id_type=MESH,
        )

    def on_ring(stream, u, step, piece, block, source, target):
        first, length = runs[stream][piece]
        ref = held_ref.at[block, u, pl.ds(first, length)]
        if source is not None:
            source = source.at[u, pl.ds(first, length)]
        index = (stream, u, step - 1, piece)
        return remote(
            ref if source is None else source, ref, send_sem.at[index], recv_sem.at[index], target
        )

    def arriving(stream, u, step, piece):
        block = place(pos + step) if stream == 1 else place(pos - step)
        return on_ring(stream, u, step, piece, block, None, left)

    def advance(u, step):
        for piece in range(2):
            for stream, target in ((0, right), (1, left)):
                if step > 0:
                    arriving(stream, u, step, piece).wait_recv()
                block = place(pos + step) if stream == 1 else place(pos - step)
                if step < n - 1:
                    source = base_ref if step == 0 else None
                    start(on_ring(stream, u, step + 1, piece, block, source, target))
                if pairs and stream == 0 and step > 0:
                    first, length = runs[0][piece]
                    ref = held_ref.at[block, u, pl.ds(first, length)]
                    index = (2, u, step - 1, piece)
                    start(remote(ref, ref, send_sem.at[index], recv_sem.at[index], partner))

    def settle(u):
        if pairs:
            for step in range(1, n):
                for piece in range(2):
                    arriving(2, u, step, piece).wait_recv()

    def choose():
        for d in range(1, n):
            block = exts_ref.at[lax.rem(k - d + n, n)]
            remote(block, block, ext_send.at[d - 1], ext_recv.at[d - 1], twin).wait_recv()
        codes = []
        for section in range(2):
            total = exts_ref[0, selected + section].astype(jnp.float32)
            for d in range(1, n):
                total = total + exts_ref[d, selected + section].astype(jnp.float32)
            codes.append(total)
        for p in range(n):
            hits = [
                [jnp.where(code[p : p + 1] == float(v), 1.0, 0.0) for v in range(variants)]
                for code in codes
            ]
            total = first_ref[0].astype(jnp.float32) * hits[0][0]
            for v in range(1, variants):
                total = total + first_ref[v].astype(jnp.float32) * hits[0][v]
            middle_ref[p] = total.astype(jnp.bfloat16)
            for part in range(2):
                total = top_ref[0, part] * hits[1][0]
                for v in range(1, variants):
                    total = total + top_ref[v, part] * hits[1][v]
                stack_ref[pl.ds((part * n + p) * half_block, half_block), :] = total
        lanes = lax.broadcasted_iota(jnp.int32, (n, dimension), 1)
        out = jnp.zeros((n, dimension), jnp.float32)
        for j in range(selected):
            rows, weights = [], []
            for picked, code, into in (
                (top_pick_ref, codes[1], rows),
                (first_pick_ref, codes[0], weights),
            ):
                total = jnp.zeros((n, dimension), jnp.float32)
                for v in range(variants):
                    hit = jnp.where(code[:n] == float(v), 1.0, 0.0)
                    total = total + hit * picked[v, j : j + 1, :]
                into.append(total)
            columns = exts_ref[:, j].reshape(dimension, dimension)
            mixed = jnp.dot(
                rows[0].astype(jnp.bfloat16), columns, preferred_element_type=jnp.float32
            )
            value = jnp.sum(mixed * weights[0], axis=1, keepdims=True)
            out = jnp.where(lanes == j, value, out)
        vals_buf[0] = out.astype(jnp.bfloat16).astype(jnp.float32) * scale

    def mix_top(u, low, high):
        def one(y, carry):
            block = held_ref[:, u, y].reshape(dimension, dimension)
            turned_ref[pl.ds(y, dimension, stride=dimension), :] = jnp.dot(
                stack_ref[...].astype(jnp.bfloat16), block, preferred_element_type=jnp.float32
            )
            return carry

        lax.fori_loop(low, high, one, 0, unroll=4)

    def mix_middle(u, low, high):
        def one(p, carry):
            matrix = middle_ref[p]
            for part in range(2):
                for w in range(half_block):
                    row = (part * n + p) * half_block + w
                    begin = pl.multiple_of(row * dimension, dimension)
                    block = turned_ref[pl.ds(begin, dimension), :].astype(jnp.bfloat16)
                    final_ref[u, part, p, w] = jnp.dot(
                        matrix, block, preferred_element_type=jnp.float32
                    ).astype(jnp.bfloat16)
            return carry

        lax.fori_loop(low, high, one, 0)

    kept = []
    quarter = n // 4

    def release(u, q):
        span = pl.ds(q * quarter, quarter)
        start(
            remote(
                final_ref.at[u, 1, span],
                arrived_ref.at[u, span],
                swap_sem.at[0, u, q],
                swap_sem.at[1, u, q],
                twin,
            )
        )
        item = pltpu.make_async_copy(
            final_ref.at[u, 0, span], kept_ref.at[u, span], kept_sem.at[u, q]
        )
        item.start()
        kept.append(item)

    for d in range(1, n):
        start(
            remote(
                ext_ref,
                exts_ref.at[k],
                ext_send.at[d - 1],
                ext_recv.at[d - 1],
                (g, lax.rem(k + d, n), c),
            )
        )
    own = pltpu.make_async_copy(base_ref, held_ref.at[k], own_sem.at[0])
    own.start()
    own_ext = pltpu.make_async_copy(ext_ref, exts_ref.at[k], own_sem.at[1])
    own_ext.start()
    advance(0, 0)
    advance(0, 1)
    own_ext.wait()
    choose()
    own.wait()
    for step in range(2, n - 1):
        advance(0, step)
    start(remote(vals_buf.at[0], vals_buf.at[1], vals_sem.at[0], vals_sem.at[1], twin))
    advance(1, 0)
    advance(0, n - 1)
    settle(0)
    work = [functools.partial(mix_top, 0, q * dimension // 4, (q + 1) * dimension // 4) for q in range(4)]
    work += [functools.partial(mix_middle, 0, q * quarter, (q + 1) * quarter) for q in range(4)]
    for step in range(1, n):
        advance(1, step)
        if work:
            work.pop(0)()
    while work:
        work.pop(0)()
    settle(1)
    for q in range(4):
        release(0, q)
    mix_top(1, 0, dimension)
    for q in range(4):
        mix_middle(1, q * quarter, (q + 1) * quarter)
        if q > 0:
            release(1, q - 1)
    remote(
        vals_buf.at[0], vals_buf.at[1], vals_sem.at[0], vals_sem.at[1], twin
    ).wait_recv()
    vals_ref[...] = vals_buf[...]
    release(1, 3)
    for u in range(2):
        for q in range(4):
            span = pl.ds(q * quarter, quarter)
            remote(
                final_ref.at[u, 1, span],
                arrived_ref.at[u, span],
                swap_sem.at[0, u, q],
                swap_sem.at[1, u, q],
                twin,
            ).wait_recv()
    for item in started:
        item.wait_send()
    for item in kept:
        item.wait()


def window(base, ext, first, top, first_pick, top_pick, n, scale):
    pairs = lax.axis_size("grp") % 2 == 0
    streams = 3 if pairs else 2
    dimension = base.shape[1]
    half_block = top.shape[2]
    state = (2, n, half_block, dimension, dimension)
    vmem = pl.BlockSpec(memory_space=pltpu.VMEM)
    hbm = pl.BlockSpec(memory_space=pl.ANY)
    return pl.pallas_call(
        functools.partial(window_kernel, n, pairs, scale),
        out_shape=[
            jax.ShapeDtypeStruct(state, jnp.bfloat16),
            jax.ShapeDtypeStruct(state, jnp.bfloat16),
            jax.ShapeDtypeStruct((2, n, dimension), jnp.float32),
        ],
        in_specs=[vmem] * 6,
        out_specs=[hbm, hbm, vmem],
        scratch_shapes=[
            pltpu.VMEM((n,) + base.shape, base.dtype),
            pltpu.VMEM((n,) + ext.shape, ext.dtype),
            pltpu.VMEM((n, dimension, dimension), jnp.bfloat16),
            pltpu.VMEM((dimension, dimension), jnp.float32),
            pltpu.VMEM((dimension * dimension, dimension), jnp.float32),
            pltpu.VMEM((2,) + state, jnp.bfloat16),
            pltpu.VMEM((2, n, dimension), jnp.float32),
            pltpu.SemaphoreType.DMA((2,)),
            pltpu.SemaphoreType.DMA((streams, 2, n - 1, 2)),
            pltpu.SemaphoreType.DMA((streams, 2, n - 1, 2)),
            pltpu.SemaphoreType.DMA((n - 1,)),
            pltpu.SemaphoreType.DMA((n - 1,)),
            pltpu.SemaphoreType.DMA((2,)),
            pltpu.SemaphoreType.DMA((2, 4)),
            pltpu.SemaphoreType.DMA((2, 2, 4)),
        ],
        compiler_params=pltpu.CompilerParams(
            collective_id=0, has_side_effects=True, vmem_limit_bytes=52 * 2**20
        ),
    )(base, ext, first, top, first_pick, top_pick)


def fused_join_kernel(paths, selected, vals_ref, core_ref, kept_ref, arrived_ref, *outs):
    dimension = kept_ref.shape[-1]
    step = 32
    for core in range(2):

        @pl.when(core_ref[0] == core)
        def _(core=core):
            for source, out, base in (
                (kept_ref, outs[core], paths * dimension),
                (arrived_ref, outs[1 - core], 0),
            ):
                for u in range(2):

                    def chunk(i, carry, source=source, out=out, base=base, u=u):
                        start = pl.multiple_of(i * step, step)
                        loaded = [
                            source[u, p, 0, pl.ds(start, step), :].astype(jnp.float32)
                            for p in range(paths)
                        ]
                        for j in range(selected):
                            total = loaded[0] * vals_ref[base + j]
                            for p in range(1, paths):
                                total = total + loaded[p] * vals_ref[base + p * dimension + j]
                            out[j, 0, u, pl.ds(start, step), :] = total
                        return carry

                    lax.fori_loop(0, dimension // step, chunk, 0)


def fused_join(vals, core, kept, arrived, selected):
    _, paths, half_block, dimension, _ = kept.shape
    spec = pl.BlockSpec((2, paths, 1, dimension, dimension), lambda w, *_: (0, 0, w, 0, 0))
    out_spec = pl.BlockSpec(
        (selected, 1, 2, dimension, dimension), lambda w, *_: (0, w, 0, 0, 0)
    )
    out = jax.ShapeDtypeStruct((selected, half_block, 2, dimension, dimension), jnp.float32)
    return pl.pallas_call(
        functools.partial(fused_join_kernel, paths, selected),
        grid_spec=pltpu.PrefetchScalarGridSpec(
            num_scalar_prefetch=2,
            grid=(half_block,),
            in_specs=[spec] * 2,
            out_specs=[out_spec] * 2,
        ),
        out_shape=[out, out],
        compiler_params=pltpu.CompilerParams(vmem_limit_bytes=50 * 2**20),
    )(vals, core, kept, arrived)


def mixes(gates, cuts, bits):
    dimension = gates.shape[-1]
    count = bits.shape[1]
    rows = lax.broadcasted_iota(jnp.int32, (dimension, dimension), 0)
    cols = lax.broadcasted_iota(jnp.int32, (dimension, dimension), 1)
    block = 2**count
    kernel = jnp.where(rows // block == cols // block, 1.0, 0.0).astype(jnp.float32)
    for k in reversed(range(count)):
        picked = jnp.where(
            (bits[:, k] == 1)[:, None, None, None], cuts[None, :, k, 1], cuts[None, :, k, 0]
        )
        low_row = rows // 2**k % 2 == 1
        low_col = cols // 2**k % 2 == 1
        entry = [[picked[:, :, a, b, None, None] for b in range(2)] for a in range(2)]
        factor = jnp.where(
            low_row,
            jnp.where(low_col, entry[1][1], entry[1][0]),
            jnp.where(low_col, entry[0][1], entry[0][0]),
        )
        kernel = kernel * factor
    return jnp.einsum(
        "hij,phjk->phik",
        gates.astype(jnp.float32),
        kernel,
        precision=lax.Precision.HIGHEST,
        preferred_element_type=jnp.float32,
    ).astype(jnp.bfloat16)


def turn_kernel(paths, half_block, states_ref, top_ref, middle_ref, out_ref, turned_ref):
    dimension = middle_ref.shape[-1]
    rows = top_ref.shape[0]

    def mix_top(y, carry):
        block = states_ref[:, 0, y].reshape(dimension, dimension)
        turned_ref[pl.ds(y, rows, stride=dimension), :] = jnp.dot(
            top_ref[...], block, preferred_element_type=jnp.float32
        )
        return carry

    lax.fori_loop(0, dimension, mix_top, 0, unroll=4)

    def mix_middle(p, carry):
        matrix = middle_ref[p]
        for side in range(2):
            for w in range(half_block):
                row = (side * paths + p) * half_block + w
                start = pl.multiple_of(row * dimension, dimension)
                block = turned_ref[pl.ds(start, dimension), :].astype(jnp.bfloat16)
                out_ref[side, p, w] = jnp.dot(
                    matrix, block, preferred_element_type=jnp.float32
                ).astype(jnp.bfloat16)
        return carry

    lax.fori_loop(0, paths, mix_middle, 0)


def turn(states, top, middle, u):
    owners, _, dimension, near, _ = states.shape
    paths = middle.shape[0]
    half_block = near // 2
    return pl.pallas_call(
        functools.partial(turn_kernel, paths, half_block),
        grid=(1,),
        in_specs=[
            pl.BlockSpec(
                (owners, 1, dimension, near, dimension),
                lambda i: (0, u, 0, 0, 0),
                pipeline_mode=pl.Buffered(1),
            ),
            pl.BlockSpec(top.shape, lambda i: (0, 0)),
            pl.BlockSpec(middle.shape, lambda i: (0, 0, 0)),
        ],
        out_specs=pl.BlockSpec(
            (2, paths, half_block, dimension, dimension), lambda i: (0, 0, 0, 0, 0)
        ),
        out_shape=jax.ShapeDtypeStruct(
            (2, paths, half_block, dimension, dimension), jnp.bfloat16
        ),
        scratch_shapes=[pltpu.VMEM((top.shape[0] * dimension, dimension), jnp.float32)],
        compiler_params=pltpu.CompilerParams(vmem_limit_bytes=50 * 2**20),
        cost_estimate=pl.CostEstimate(
            flops=4 * top.shape[0] * dimension**3,
            bytes_accessed=4 * dimension**3 * 2,
            transcendentals=0,
        ),
    )(states, top, middle)


def join_kernel(paths, selected, vals_ref, *refs):
    mine = refs[:2]
    other = refs[2:4]
    outs = refs[4:]
    c = vals_ref[2 * paths * selected]
    dimension = mine[0].shape[-1]
    step = 32

    for u in range(2):
        for source, which in ((mine[u], 0), (other[u], 1)):
            half = c if which == 0 else 1.0 - c
            for h in range(2):

                @pl.when(half == float(h))
                def _(source=source, h=h, u=u):
                    def chunk(i, carry):
                        start = pl.multiple_of(i * step, step)
                        loaded = [
                            source[p, 0, pl.ds(start, step), :].astype(jnp.float32)
                            for p in range(paths)
                        ]
                        for j in range(selected):
                            base = (1 - h) * paths * selected + j
                            total = loaded[0] * vals_ref[base]
                            for p in range(1, paths):
                                total = total + loaded[p] * vals_ref[base + p * selected]
                            outs[h][j, 0, u, pl.ds(start, step), :] = total
                        return carry

                    lax.fori_loop(0, dimension // step, chunk, 0)


def join(vals, mine, other):
    paths, half_block, dimension, _ = mine[0].shape
    selected = vals.shape[0] // (2 * paths)
    spec = pl.BlockSpec((paths, 1, dimension, dimension), lambda w, *_: (0, w, 0, 0))
    out_spec = pl.BlockSpec(
        (selected, 1, 2, dimension, dimension), lambda w, *_: (0, w, 0, 0, 0)
    )
    out = jax.ShapeDtypeStruct((selected, half_block, 2, dimension, dimension), jnp.float32)
    return pl.pallas_call(
        functools.partial(join_kernel, paths, selected),
        grid_spec=pltpu.PrefetchScalarGridSpec(
            num_scalar_prefetch=1,
            grid=(half_block,),
            in_specs=[spec] * 4,
            out_specs=[out_spec] * 2,
        ),
        out_shape=[out, out],
        compiler_params=pltpu.CompilerParams(vmem_limit_bytes=50 * 2**20),
    )(vals, *mine, *other)


def body_fused(base, block_gates, cut_ops, path_bits, own_picks):
    sections = path_bits.shape[1] // 2
    c, k, owners = lax.axis_index("state"), lax.axis_index("path"), lax.axis_size("path")
    dimension = base.shape[-1]
    near = base.shape[2]
    half_block = near // 2
    selected = own_picks.shape[0]
    variants = 2**sections
    powers = 2 ** jnp.arange(sections, dtype=jnp.int32)
    every = jnp.arange(variants, dtype=jnp.int32)[:, None] // powers[None, :] % 2

    def of_half(block, cuts):
        gates = lax.dynamic_index_in_dim(block, c, 0, keepdims=True)
        ops = lax.dynamic_index_in_dim(cuts, c, 0, keepdims=True)
        return mixes(gates, ops, every)[:, 0]

    first = of_half(block_gates[1], cut_ops[:, :sections])
    top = of_half(block_gates[2], cut_ops[:, sections:])
    top = jnp.transpose(
        top.reshape(variants, dimension, 2, owners, half_block), (0, 1, 3, 2, 4)
    ).reshape(variants, dimension, dimension)
    own_rows = top.reshape(variants, 2, owners, half_block, dimension)
    own_rows = lax.dynamic_index_in_dim(own_rows, k, 2, keepdims=False)
    own_rows = jnp.where(c == 1, own_rows[:, ::-1], own_rows).astype(jnp.float32)

    every_lane = jnp.arange(dimension)
    z_hot = (own_picks[:, None] % dimension == every_lane).astype(jnp.bfloat16)
    y_hot = (own_picks[:, None] // dimension % dimension == every_lane).astype(jnp.bfloat16)
    w_hot = (own_picks[:, None] // (dimension * dimension) // 2 == every_lane).astype(jnp.bfloat16)
    first_pick = jnp.einsum("jy,pyk->pjk", y_hot, first, preferred_element_type=jnp.float32)
    top_pick = jnp.einsum("jw,pwv->pjv", w_hot, top, preferred_element_type=jnp.float32)
    lanes = jnp.einsum("jz,uyvz->juvy", z_hot, base, preferred_element_type=jnp.float32)
    u_own = own_picks // (dimension * dimension) % 2
    columns = jnp.where(u_own[:, None, None] == 1, lanes[:, 1], lanes[:, 0]).astype(jnp.bfloat16)
    codes = jnp.sum(path_bits.reshape(2, sections) * powers[None, :], axis=1)
    spot = jnp.arange(near)[None, :, None] == k
    marks = jnp.where(spot, codes[:, None, None], 0).astype(jnp.bfloat16)
    ext = jnp.concatenate([columns, jnp.broadcast_to(marks, (2, near, dimension))], axis=0)

    kept, arrived, vals = window(
        base, ext, first, own_rows, first_pick, top_pick, owners, 1.0 / math.sqrt(owners)
    )
    outs = fused_join(vals.reshape(-1), c[None].astype(jnp.int32), kept, arrived, selected)
    return tuple(out.reshape(selected, 1, near, dimension, dimension) for out in outs)


def body(start_states, block_gates, cut_ops, path_bits, left_pick, right_pick):
    sections = path_bits.shape[1] // 2
    c = lax.axis_index("state")
    k = lax.axis_index("path")
    owners = lax.axis_size("path")
    dimension = start_states.shape[-1]
    half_block = dimension // (2 * owners)
    near = 2 * half_block
    per_device = path_bits.shape[0]
    paths = owners * per_device
    selected = left_pick.shape[0]

    mine = lax.all_to_all(start_states, "state", split_axis=0, concat_axis=1, tiled=True)
    mine = mine.reshape(2, half_block, 2, dimension, dimension)
    laid = jnp.transpose(mine, (2, 3, 0, 1, 4)).reshape(2, dimension, near, dimension)
    gate = lax.dynamic_index_in_dim(block_gates[0], c, 0, keepdims=False)
    base = jnp.einsum(
        "uyvz,iz->uyvi", laid, gate, preferred_element_type=jnp.float32
    ).astype(jnp.bfloat16)

    picks = jnp.stack([left_pick, right_pick])
    own_picks = lax.dynamic_index_in_dim(picks, c, 0, keepdims=False)
    if per_device == 1 and owners % 4 == 0 and owners <= 8 and near % 16 == 0:
        return body_fused(base, block_gates, cut_ops, path_bits, own_picks)

    z_hot = (own_picks[:, None] % dimension == jnp.arange(dimension)[None, :]).astype(jnp.bfloat16)
    lanes = jnp.einsum("jz,uyvz->juyv", z_hot, base, preferred_element_type=jnp.float32)
    u_own = own_picks // (dimension * dimension) % 2
    near_pick = jnp.where(u_own[:, None, None] == 1, lanes[:, 1], lanes[:, 0])
    small = jnp.concatenate(
        [
            near_pick.astype(jnp.bfloat16).reshape(-1),
            jnp.pad(path_bits.astype(jnp.bfloat16), ((0, 0), (0, dimension - 2 * sections))).reshape(-1),
        ]
    )
    pooled = lax.all_gather(small, ("path", "state"), axis=0)
    size = selected * dimension * near
    bits = pooled[:, size:].reshape(owners, 2, per_device, dimension)[:, 0, :, : 2 * sections]
    bits = bits.reshape(paths, 2 * sections).astype(jnp.int32)
    columns = pooled[:, :size].reshape(owners, 2, selected, dimension, near)

    gathered = lax.all_gather(base, "path", axis=0)

    mix1 = mixes(block_gates[1], cut_ops[:, :sections], bits[:, :sections])
    mix2 = mixes(block_gates[2], cut_ops[:, sections:], bits[:, sections:])
    turned2 = jnp.transpose(
        mix2.reshape(paths, 2, dimension, 2, owners, half_block), (0, 1, 2, 4, 3, 5)
    ).reshape(paths, 2, dimension, dimension)

    row_y = picks // dimension % dimension
    row_w = picks // (dimension * dimension) // 2
    y_hot = (row_y[:, :, None] == jnp.arange(dimension)).astype(jnp.bfloat16)
    w_hot = (row_w[:, :, None] == jnp.arange(dimension)).astype(jnp.bfloat16)
    m1_rows = jnp.einsum("hjy,phyk->phjk", y_hot, mix1, preferred_element_type=jnp.float32)
    m2_rows = jnp.einsum("hjw,phwv->phjv", w_hot, turned2, preferred_element_type=jnp.float32)
    cols = jnp.transpose(columns, (1, 2, 3, 0, 4)).reshape(2, selected, dimension, dimension)
    first = jnp.einsum(
        "phjy,hjyv->phjv",
        m1_rows.astype(jnp.bfloat16),
        cols,
        preferred_element_type=jnp.float32,
    ).astype(jnp.bfloat16)
    vals = jnp.sum(first.astype(jnp.float32) * m2_rows, axis=-1).astype(jnp.bfloat16)
    scale = 1.0 / math.sqrt(paths)
    flat = jnp.transpose(vals.astype(jnp.float32) * scale, (1, 0, 2)).reshape(-1)
    flat = jnp.concatenate([flat, c.astype(jnp.float32)[None]])

    own2 = lax.dynamic_index_in_dim(turned2, c, 1, keepdims=False)
    own2 = own2.reshape(paths, 2, owners, half_block, dimension)
    own2 = lax.dynamic_index_in_dim(own2, k, 2, keepdims=False)
    own2 = jnp.where(c == 1, own2[:, ::-1], own2)
    top = jnp.transpose(own2, (1, 0, 2, 3)).reshape(2 * paths * half_block, dimension)
    middle = lax.dynamic_index_in_dim(mix1, c, 1, keepdims=False)

    kept, arrived = [], []
    for u in range(2):
        both = turn(gathered, top, middle, u)
        kept.append(both[0])
        arrived.append(lax.ppermute(both[1], "state", [(0, 1), (1, 0)]))
    outs = join(flat, kept, arrived)
    return tuple(out.reshape(selected, 1, near, dimension, dimension) for out in outs)


def solution(mesh):
    in_specs = (P(None, "state", "path", None, None), P(), P(), P(("grp", "path"), None), P(), P())
    out_specs = (P("grp", "state", "path", None, None), P("grp", "state", "path", None, None))
    return jax.shard_map(body, mesh=mesh, in_specs=in_specs, out_specs=out_specs, check_vma=False)
```

```python
import functools
import math

import jax
import jax.numpy as jnp
from jax import lax
from jax.experimental import pallas as pl
from jax.experimental.pallas import tpu as pltpu
from jax.sharding import PartitionSpec as P


MESH = pl.DeviceIdType.MESH


def window_kernel(
    n,
    pairs,
    scale,
    half_block,
    base_ref,
    ext_ref,
    first_ref,
    top_ref,
    kept_ref,
    arrived_ref,
    vals_ref,
    held_ref,
    exts_ref,
    middle_ref,
    stack_ref,
    packed_ref,
    turned_ref,
    final_ref,
    vals_buf,
    own_sem,
    send_sem,
    recv_sem,
    ext_send,
    ext_recv,
    vals_sem,
    kept_sem,
    swap_sem,
):
    g, k, c = lax.axis_index("grp"), lax.axis_index("path"), lax.axis_index("state")
    dimension = base_ref.shape[1]
    variants = top_ref.shape[0]
    selected = top_ref.shape[1] - 2 * half_block
    odd = lax.rem(k, 2)
    pos = (1 - odd) * (k // 2) + odd * (n - 1 - k // 2)

    def place(p):
        p = lax.rem(p + n, n)
        high = p // (n // 2)
        return (1 - high) * (2 * p) + high * (2 * (n - 1 - p) + 1)

    right, left = (g, place(pos + 1), c), (g, place(pos - 1), c)
    side = lax.rem(g, 2) if pairs else 0
    partner = (g + 1 - 2 * side, k, c)
    twin = (g, k, 1 - c)

    barrier = pltpu.get_barrier_semaphore()
    greeted = [(g, lax.rem(k + d, n), c) for d in range(1, n)] + [twin]
    if pairs:
        greeted.append(partner)
    for other in greeted:
        pl.semaphore_signal(barrier, inc=1, device_id=other, device_id_type=MESH)
    pl.semaphore_wait(barrier, len(greeted))

    outer = (dimension + 2) // 3 if pairs else dimension // 2
    middle = dimension - 2 * outer if pairs else dimension - outer

    def cut(start, length):
        half = (length + 1) // 2
        return ((start, half), (start + half, length - half))

    far = dimension - outer
    runs = (
        cut(side * far if pairs else 0, outer),
        cut(outer, middle),
        cut((1 - side) * far if pairs else 0, outer),
    )

    started = []

    def start(item):
        item.start()
        started.append(item)

    def remote(source, target_ref, send, recv, device):
        return pltpu.make_async_remote_copy(
            src_ref=source,
            dst_ref=target_ref,
            send_sem=send,
            recv_sem=recv,
            device_id=device,
            device_id_type=MESH,
        )

    def on_ring(stream, u, step, piece, block, source, target):
        first, length = runs[stream][piece]
        ref = held_ref.at[block, u, pl.ds(first, length)]
        if source is not None:
            source = source.at[u, pl.ds(first, length)]
        index = (stream, u, step - 1, piece)
        return remote(
            ref if source is None else source, ref, send_sem.at[index], recv_sem.at[index], target
        )

    def arriving(stream, u, step, piece):
        block = place(pos + step) if stream == 1 else place(pos - step)
        return on_ring(stream, u, step, piece, block, None, left)

    work = []

    def advance(u, step):
        for piece in range(2):
            if work and u == 1:
                work.pop(0)()
            for stream, target in ((0, right), (1, left)):
                if step > 0:
                    arriving(stream, u, step, piece).wait_recv()
                block = place(pos + step) if stream == 1 else place(pos - step)
                if step < n - 1:
                    source = base_ref if step == 0 else None
                    start(on_ring(stream, u, step + 1, piece, block, source, target))
                if pairs and stream == 0 and step > 0:
                    first, length = runs[0][piece]
                    ref = held_ref.at[block, u, pl.ds(first, length)]
                    index = (2, u, step - 1, piece)
                    start(remote(ref, ref, send_sem.at[index], recv_sem.at[index], partner))

    def settle(u):
        if pairs:
            for step in range(1, n):
                for piece in range(2):
                    arriving(2, u, step, piece).wait_recv()

    def choose():
        for d in range(1, n):
            block = exts_ref.at[lax.rem(k - d + n, n)]
            remote(block, block, ext_send.at[d - 1], ext_recv.at[d - 1], twin).wait_recv()
        codes = []
        for section in range(2):
            total = exts_ref[0, selected + section].astype(jnp.float32)
            for d in range(1, n):
                total = total + exts_ref[d, selected + section].astype(jnp.float32)
            codes.append(total)
        for p in range(n):
            hits = [
                [jnp.where(code[p : p + 1] == float(v), 1.0, 0.0) for v in range(variants)]
                for code in codes
            ]
            total = first_ref[0, :dimension] * hits[0][0]
            for v in range(1, variants):
                total = total + first_ref[v, :dimension] * hits[0][v]
            middle_ref[p] = total.astype(jnp.bfloat16)
            for part in range(2):
                span = slice(part * half_block, (part + 1) * half_block)
                total = top_ref[0, span] * hits[1][0]
                for v in range(1, variants):
                    total = total + top_ref[v, span] * hits[1][v]
                stack_ref[pl.ds((part * n + p) * half_block, half_block), :] = total
        packed_ref[...] = stack_ref[...].astype(jnp.bfloat16)
        lanes = lax.broadcasted_iota(jnp.int32, (n, dimension), 1)
        out = jnp.zeros((n, dimension), jnp.float32)
        for j in range(selected):
            rows, weights = [], []
            for picked, at, code, into in (
                (top_ref, 2 * half_block + j, codes[1], rows),
                (first_ref, dimension + j, codes[0], weights),
            ):
                total = jnp.zeros((n, dimension), jnp.float32)
                for v in range(variants):
                    hit = jnp.where(code[:n] == float(v), 1.0, 0.0)
                    total = total + hit * picked[v, at : at + 1, :]
                into.append(total)
            columns = exts_ref[:, j].reshape(dimension, dimension)
            mixed = jnp.dot(
                rows[0].astype(jnp.bfloat16), columns, preferred_element_type=jnp.float32
            )
            value = jnp.sum(mixed * weights[0], axis=1, keepdims=True)
            out = jnp.where(lanes == j, value, out)
        vals_buf[0] = out.astype(jnp.bfloat16).astype(jnp.float32) * scale

    def mix_top(u, low, high):
        def one(i, carry):
            blocks = [held_ref[:, u, 2 * i + e].reshape(dimension, dimension) for e in range(2)]
            mixed = jnp.dot(
                packed_ref[...],
                jnp.concatenate(blocks, axis=1),
                preferred_element_type=jnp.float32,
            )
            for e in range(2):
                turned_ref[pl.ds(2 * i + e, dimension, stride=dimension), :] = mixed[
                    :, e * dimension : (e + 1) * dimension
                ]
            return carry

        lax.fori_loop(low // 2, high // 2, one, 0, unroll=2)

    def mix_middle(u, low, high):
        def one(p, carry):
            matrix = middle_ref[p]
            for part in range(2):
                for w in range(0, half_block, 2):
                    row = (part * n + p) * half_block + w
                    begin = pl.multiple_of(row * dimension, dimension)
                    blocks = [
                        turned_ref[pl.ds(begin + e * dimension, dimension), :].astype(jnp.bfloat16)
                        for e in range(2)
                    ]
                    mixed = jnp.dot(
                        matrix,
                        jnp.concatenate(blocks, axis=1),
                        preferred_element_type=jnp.float32,
                    ).astype(jnp.bfloat16)
                    for e in range(2):
                        final_ref[u, part, p, w + e] = mixed[:, e * dimension : (e + 1) * dimension]
            return carry

        lax.fori_loop(low, high, one, 0)

    kept = []
    quarter = n // 4

    def release(u, q):
        span = pl.ds(q * quarter, quarter)
        start(
            remote(
                final_ref.at[u, 1, span],
                arrived_ref.at[u, span],
                swap_sem.at[0, u, q],
                swap_sem.at[1, u, q],
                twin,
            )
        )
        item = pltpu.make_async_copy(
            final_ref.at[u, 0, span], kept_ref.at[u, span], kept_sem.at[u, q]
        )
        item.start()
        kept.append(item)

    for d in range(1, n):
        start(
            remote(
                ext_ref,
                exts_ref.at[k],
                ext_send.at[d - 1],
                ext_recv.at[d - 1],
                (g, lax.rem(k + d, n), c),
            )
        )
    own = pltpu.make_async_copy(base_ref, held_ref.at[k], own_sem.at[0])
    own.start()
    own_ext = pltpu.make_async_copy(ext_ref, exts_ref.at[k], own_sem.at[1])
    own_ext.start()
    advance(0, 0)
    advance(0, 1)
    own_ext.wait()
    choose()
    own.wait()
    for step in range(2, n - 1):
        advance(0, step)
    start(remote(vals_buf.at[0], vals_buf.at[1], vals_sem.at[0], vals_sem.at[1], twin))
    advance(1, 0)
    advance(0, n - 1)
    settle(0)
    for q in range(8):
        work.append(functools.partial(mix_top, 0, q * dimension // 8, (q + 1) * dimension // 8))
    for q in range(n):
        work.append(functools.partial(mix_middle, 0, q, q + 1))
    for step in range(1, n):
        advance(1, step)
    while work:
        work.pop(0)()
    settle(1)
    for q in range(4):
        release(0, q)
    mix_top(1, 0, dimension)
    for q in range(4):
        mix_middle(1, q * quarter, (q + 1) * quarter)
        if q > 0:
            release(1, q - 1)
    remote(
        vals_buf.at[0], vals_buf.at[1], vals_sem.at[0], vals_sem.at[1], twin
    ).wait_recv()
    vals_ref[...] = vals_buf[...]
    release(1, 3)
    for u in range(2):
        for q in range(4):
            span = pl.ds(q * quarter, quarter)
            remote(
                final_ref.at[u, 1, span],
                arrived_ref.at[u, span],
                swap_sem.at[0, u, q],
                swap_sem.at[1, u, q],
                twin,
            ).wait_recv()
    for item in started:
        item.wait_send()
    for item in kept:
        item.wait()


def window(base, ext, first, top, half_block, n, scale):
    pairs = lax.axis_size("grp") % 2 == 0
    streams = 3 if pairs else 2
    dimension = base.shape[1]
    state = (2, n, half_block, dimension, dimension)
    vmem = pl.BlockSpec(memory_space=pltpu.VMEM)
    hbm = pl.BlockSpec(memory_space=pl.ANY)
    return pl.pallas_call(
        functools.partial(window_kernel, n, pairs, scale, half_block),
        out_shape=[
            jax.ShapeDtypeStruct(state, jnp.bfloat16),
            jax.ShapeDtypeStruct(state, jnp.bfloat16),
            jax.ShapeDtypeStruct((2, n, dimension), jnp.float32),
        ],
        in_specs=[vmem] * 4,
        out_specs=[hbm, hbm, vmem],
        scratch_shapes=[
            pltpu.VMEM((n,) + base.shape, base.dtype),
            pltpu.VMEM((n,) + ext.shape, ext.dtype),
            pltpu.VMEM((n, dimension, dimension), jnp.bfloat16),
            pltpu.VMEM((dimension, dimension), jnp.float32),
            pltpu.VMEM((dimension, dimension), jnp.bfloat16),
            pltpu.VMEM((dimension * dimension, dimension), jnp.float32),
            pltpu.VMEM((2,) + state, jnp.bfloat16),
            pltpu.VMEM((2, n, dimension), jnp.float32),
            pltpu.SemaphoreType.DMA((2,)),
            pltpu.SemaphoreType.DMA((streams, 2, n - 1, 2)),
            pltpu.SemaphoreType.DMA((streams, 2, n - 1, 2)),
            pltpu.SemaphoreType.DMA((n - 1,)),
            pltpu.SemaphoreType.DMA((n - 1,)),
            pltpu.SemaphoreType.DMA((2,)),
            pltpu.SemaphoreType.DMA((2, 4)),
            pltpu.SemaphoreType.DMA((2, 2, 4)),
        ],
        compiler_params=pltpu.CompilerParams(
            collective_id=0, has_side_effects=True, vmem_limit_bytes=52 * 2**20
        ),
    )(base, ext, first, top)


def fused_join_kernel(paths, selected, vals_ref, core_ref, kept_ref, arrived_ref, *outs):
    dimension = kept_ref.shape[-1]
    step = 32
    for core in range(2):

        @pl.when(core_ref[0] == core)
        def _(core=core):
            for source, out, base in (
                (kept_ref, outs[core], paths * dimension),
                (arrived_ref, outs[1 - core], 0),
            ):
                for u in range(2):

                    def chunk(i, carry, source=source, out=out, base=base, u=u):
                        start = pl.multiple_of(i * step, step)
                        loaded = [
                            source[u, p, 0, pl.ds(start, step), :].astype(jnp.float32)
                            for p in range(paths)
                        ]
                        for j in range(selected):
                            total = loaded[0] * vals_ref[base + j]
                            for p in range(1, paths):
                                total = total + loaded[p] * vals_ref[base + p * dimension + j]
                            out[j, 0, u, pl.ds(start, step), :] = total
                        return carry

                    lax.fori_loop(0, dimension // step, chunk, 0)


def fused_join(vals, core, kept, arrived, selected):
    _, paths, half_block, dimension, _ = kept.shape
    spec = pl.BlockSpec((2, paths, 1, dimension, dimension), lambda w, *_: (0, 0, w, 0, 0))
    out_spec = pl.BlockSpec(
        (selected, 1, 2, dimension, dimension), lambda w, *_: (0, w, 0, 0, 0)
    )
    out = jax.ShapeDtypeStruct((selected, half_block, 2, dimension, dimension), jnp.float32)
    return pl.pallas_call(
        functools.partial(fused_join_kernel, paths, selected),
        grid_spec=pltpu.PrefetchScalarGridSpec(
            num_scalar_prefetch=2,
            grid=(half_block,),
            in_specs=[spec] * 2,
            out_specs=[out_spec] * 2,
        ),
        out_shape=[out, out],
        compiler_params=pltpu.CompilerParams(vmem_limit_bytes=50 * 2**20),
    )(vals, core, kept, arrived)


def mixes(gates, cuts, bits, columns=None):
    dimension = gates.shape[-1]
    count = bits.shape[1]
    rows = lax.broadcasted_iota(jnp.int32, (dimension, dimension), 0)
    cols = lax.broadcasted_iota(jnp.int32, (dimension, dimension), 1)
    if columns is not None:
        cols = columns(cols)
    block = 2**count
    kernel = jnp.where(rows // block == cols // block, 1.0, 0.0).astype(jnp.float32)
    for k in reversed(range(count)):
        picked = jnp.where(
            (bits[:, k] == 1)[:, None, None, None], cuts[None, :, k, 1], cuts[None, :, k, 0]
        )
        low_row = rows // 2**k % 2 == 1
        low_col = cols // 2**k % 2 == 1
        entry = [[picked[:, :, a, b, None, None] for b in range(2)] for a in range(2)]
        factor = jnp.where(
            low_row,
            jnp.where(low_col, entry[1][1], entry[1][0]),
            jnp.where(low_col, entry[0][1], entry[0][0]),
        )
        kernel = kernel * factor
    return jnp.einsum(
        "hij,phjk->phik",
        gates.astype(jnp.float32),
        kernel,
        precision=lax.Precision.HIGHEST,
        preferred_element_type=jnp.float32,
    ).astype(jnp.bfloat16)


def turn_kernel(paths, half_block, states_ref, top_ref, middle_ref, out_ref, turned_ref):
    dimension = middle_ref.shape[-1]
    rows = top_ref.shape[0]

    def mix_top(y, carry):
        block = states_ref[:, 0, y].reshape(dimension, dimension)
        turned_ref[pl.ds(y, rows, stride=dimension), :] = jnp.dot(
            top_ref[...], block, preferred_element_type=jnp.float32
        )
        return carry

    lax.fori_loop(0, dimension, mix_top, 0, unroll=4)

    def mix_middle(p, carry):
        matrix = middle_ref[p]
        for side in range(2):
            for w in range(half_block):
                row = (side * paths + p) * half_block + w
                start = pl.multiple_of(row * dimension, dimension)
                block = turned_ref[pl.ds(start, dimension), :].astype(jnp.bfloat16)
                out_ref[side, p, w] = jnp.dot(
                    matrix, block, preferred_element_type=jnp.float32
                ).astype(jnp.bfloat16)
        return carry

    lax.fori_loop(0, paths, mix_middle, 0)


def turn(states, top, middle, u):
    owners, _, dimension, near, _ = states.shape
    paths = middle.shape[0]
    half_block = near // 2
    return pl.pallas_call(
        functools.partial(turn_kernel, paths, half_block),
        grid=(1,),
        in_specs=[
            pl.BlockSpec(
                (owners, 1, dimension, near, dimension),
                lambda i: (0, u, 0, 0, 0),
                pipeline_mode=pl.Buffered(1),
            ),
            pl.BlockSpec(top.shape, lambda i: (0, 0)),
            pl.BlockSpec(middle.shape, lambda i: (0, 0, 0)),
        ],
        out_specs=pl.BlockSpec(
            (2, paths, half_block, dimension, dimension), lambda i: (0, 0, 0, 0, 0)
        ),
        out_shape=jax.ShapeDtypeStruct(
            (2, paths, half_block, dimension, dimension), jnp.bfloat16
        ),
        scratch_shapes=[pltpu.VMEM((top.shape[0] * dimension, dimension), jnp.float32)],
        compiler_params=pltpu.CompilerParams(vmem_limit_bytes=50 * 2**20),
        cost_estimate=pl.CostEstimate(
            flops=4 * top.shape[0] * dimension**3,
            bytes_accessed=4 * dimension**3 * 2,
            transcendentals=0,
        ),
    )(states, top, middle)


def join_kernel(paths, selected, vals_ref, *refs):
    mine = refs[:2]
    other = refs[2:4]
    outs = refs[4:]
    c = vals_ref[2 * paths * selected]
    dimension = mine[0].shape[-1]
    step = 32

    for u in range(2):
        for source, which in ((mine[u], 0), (other[u], 1)):
            half = c if which == 0 else 1.0 - c
            for h in range(2):

                @pl.when(half == float(h))
                def _(source=source, h=h, u=u):
                    def chunk(i, carry):
                        start = pl.multiple_of(i * step, step)
                        loaded = [
                            source[p, 0, pl.ds(start, step), :].astype(jnp.float32)
                            for p in range(paths)
                        ]
                        for j in range(selected):
                            base = (1 - h) * paths * selected + j
                            total = loaded[0] * vals_ref[base]
                            for p in range(1, paths):
                                total = total + loaded[p] * vals_ref[base + p * selected]
                            outs[h][j, 0, u, pl.ds(start, step), :] = total
                        return carry

                    lax.fori_loop(0, dimension // step, chunk, 0)


def join(vals, mine, other):
    paths, half_block, dimension, _ = mine[0].shape
    selected = vals.shape[0] // (2 * paths)
    spec = pl.BlockSpec((paths, 1, dimension, dimension), lambda w, *_: (0, w, 0, 0))
    out_spec = pl.BlockSpec(
        (selected, 1, 2, dimension, dimension), lambda w, *_: (0, w, 0, 0, 0)
    )
    out = jax.ShapeDtypeStruct((selected, half_block, 2, dimension, dimension), jnp.float32)
    return pl.pallas_call(
        functools.partial(join_kernel, paths, selected),
        grid_spec=pltpu.PrefetchScalarGridSpec(
            num_scalar_prefetch=1,
            grid=(half_block,),
            in_specs=[spec] * 4,
            out_specs=[out_spec] * 2,
        ),
        out_shape=[out, out],
        compiler_params=pltpu.CompilerParams(vmem_limit_bytes=50 * 2**20),
    )(vals, *mine, *other)


def body_fused(base, block_gates, cut_ops, path_bits, own_picks):
    sections = path_bits.shape[1] // 2
    c, k, owners = lax.axis_index("state"), lax.axis_index("path"), lax.axis_size("path")
    dimension = base.shape[-1]
    near = base.shape[2]
    half_block = near // 2
    selected = own_picks.shape[0]
    variants = 2**sections
    powers = 2 ** jnp.arange(sections, dtype=jnp.int32)
    every = jnp.arange(variants, dtype=jnp.int32)[:, None] // powers[None, :] % 2

    def of_half(array):
        return lax.dynamic_index_in_dim(array, c, 0, keepdims=False)

    every_lane = jnp.arange(dimension)
    z_hot = (own_picks[:, None] % dimension == every_lane).astype(jnp.bfloat16)
    y_hot = (own_picks[:, None] // dimension % dimension == every_lane).astype(jnp.bfloat16)
    w_hot = (own_picks[:, None] // (dimension * dimension) // 2 == every_lane).astype(jnp.bfloat16)
    second, third = of_half(block_gates[1]), of_half(block_gates[2])
    ops = of_half(cut_ops)

    def picked(hot, gate):
        return jnp.dot(hot, gate, preferred_element_type=jnp.float32).astype(jnp.bfloat16)

    first = mixes(
        jnp.concatenate([second, picked(y_hot, second)])[None], ops[None, :sections], every
    )[:, 0].astype(jnp.float32)

    def columns_of(q):
        return q // half_block % 2 * (dimension // 2) + q // near * half_block + q % half_block

    rows = third.reshape(2, owners, half_block, dimension)
    rows = lax.dynamic_index_in_dim(rows, k, 1, keepdims=False)
    rows = jnp.where(c == 1, rows[::-1], rows).reshape(near, dimension)
    top = mixes(
        jnp.concatenate([rows, picked(w_hot, third)])[None], ops[None, sections:], every, columns_of
    )[:, 0].astype(jnp.float32)

    lanes = jnp.einsum("jz,uyvz->juvy", z_hot, base, preferred_element_type=jnp.float32)
    u_own = own_picks // (dimension * dimension) % 2
    columns = jnp.where(u_own[:, None, None] == 1, lanes[:, 1], lanes[:, 0]).astype(jnp.bfloat16)
    codes = jnp.sum(path_bits.reshape(2, sections) * powers[None, :], axis=1)
    spot = jnp.arange(near)[None, :, None] == k
    marks = jnp.where(spot, codes[:, None, None], 0).astype(jnp.bfloat16)
    ext = jnp.concatenate([columns, jnp.broadcast_to(marks, (2, near, dimension))], axis=0)

    kept, arrived, vals = window(
        base, ext, first, top, half_block, owners, 1.0 / math.sqrt(owners)
    )
    outs = fused_join(vals.reshape(-1), c[None].astype(jnp.int32), kept, arrived, selected)
    return tuple(out.reshape(selected, 1, near, dimension, dimension) for out in outs)


def body(start_states, block_gates, cut_ops, path_bits, left_pick, right_pick):
    sections = path_bits.shape[1] // 2
    c = lax.axis_index("state")
    k = lax.axis_index("path")
    owners = lax.axis_size("path")
    dimension = start_states.shape[-1]
    half_block = dimension // (2 * owners)
    near = 2 * half_block
    per_device = path_bits.shape[0]
    paths = owners * per_device
    selected = left_pick.shape[0]

    mine = lax.all_to_all(start_states, "state", split_axis=0, concat_axis=1, tiled=True)
    mine = mine.reshape(2, half_block, 2, dimension, dimension)
    laid = jnp.transpose(mine, (2, 3, 0, 1, 4)).reshape(2, dimension, near, dimension)
    gate = lax.dynamic_index_in_dim(block_gates[0], c, 0, keepdims=False)
    base = jnp.einsum(
        "uyvz,iz->uyvi", laid, gate, preferred_element_type=jnp.float32
    ).astype(jnp.bfloat16)

    picks = jnp.stack([left_pick, right_pick])
    own_picks = lax.dynamic_index_in_dim(picks, c, 0, keepdims=False)
    if per_device == 1 and owners % 4 == 0 and owners <= 8 and near % 16 == 0:
        return body_fused(base, block_gates, cut_ops, path_bits, own_picks)

    z_hot = (own_picks[:, None] % dimension == jnp.arange(dimension)[None, :]).astype(jnp.bfloat16)
    lanes = jnp.einsum("jz,uyvz->juyv", z_hot, base, preferred_element_type=jnp.float32)
    u_own = own_picks // (dimension * dimension) % 2
    near_pick = jnp.where(u_own[:, None, None] == 1, lanes[:, 1], lanes[:, 0])
    small = jnp.concatenate(
        [
            near_pick.astype(jnp.bfloat16).reshape(-1),
            jnp.pad(path_bits.astype(jnp.bfloat16), ((0, 0), (0, dimension - 2 * sections))).reshape(-1),
        ]
    )
    pooled = lax.all_gather(small, ("path", "state"), axis=0)
    size = selected * dimension * near
    bits = pooled[:, size:].reshape(owners, 2, per_device, dimension)[:, 0, :, : 2 * sections]
    bits = bits.reshape(paths, 2 * sections).astype(jnp.int32)
    columns = pooled[:, :size].reshape(owners, 2, selected, dimension, near)

    gathered = lax.all_gather(base, "path", axis=0)

    mix1 = mixes(block_gates[1], cut_ops[:, :sections], bits[:, :sections])
    mix2 = mixes(block_gates[2], cut_ops[:, sections:], bits[:, sections:])
    turned2 = jnp.transpose(
        mix2.reshape(paths, 2, dimension, 2, owners, half_block), (0, 1, 2, 4, 3, 5)
    ).reshape(paths, 2, dimension, dimension)

    row_y = picks // dimension % dimension
    row_w = picks // (dimension * dimension) // 2
    y_hot = (row_y[:, :, None] == jnp.arange(dimension)).astype(jnp.bfloat16)
    w_hot = (row_w[:, :, None] == jnp.arange(dimension)).astype(jnp.bfloat16)
    m1_rows = jnp.einsum("hjy,phyk->phjk", y_hot, mix1, preferred_element_type=jnp.float32)
    m2_rows = jnp.einsum("hjw,phwv->phjv", w_hot, turned2, preferred_element_type=jnp.float32)
    cols = jnp.transpose(columns, (1, 2, 3, 0, 4)).reshape(2, selected, dimension, dimension)
    first = jnp.einsum(
        "phjy,hjyv->phjv",
        m1_rows.astype(jnp.bfloat16),
        cols,
        preferred_element_type=jnp.float32,
    ).astype(jnp.bfloat16)
    vals = jnp.sum(first.astype(jnp.float32) * m2_rows, axis=-1).astype(jnp.bfloat16)
    scale = 1.0 / math.sqrt(paths)
    flat = jnp.transpose(vals.astype(jnp.float32) * scale, (1, 0, 2)).reshape(-1)
    flat = jnp.concatenate([flat, c.astype(jnp.float32)[None]])

    own2 = lax.dynamic_index_in_dim(turned2, c, 1, keepdims=False)
    own2 = own2.reshape(paths, 2, owners, half_block, dimension)
    own2 = lax.dynamic_index_in_dim(own2, k, 2, keepdims=False)
    own2 = jnp.where(c == 1, own2[:, ::-1], own2)
    top = jnp.transpose(own2, (1, 0, 2, 3)).reshape(2 * paths * half_block, dimension)
    middle = lax.dynamic_index_in_dim(mix1, c, 1, keepdims=False)

    kept, arrived = [], []
    for u in range(2):
        both = turn(gathered, top, middle, u)
        kept.append(both[0])
        arrived.append(lax.ppermute(both[1], "state", [(0, 1), (1, 0)]))
    outs = join(flat, kept, arrived)
    return tuple(out.reshape(selected, 1, near, dimension, dimension) for out in outs)


def solution(mesh):
    in_specs = (P(None, "state", "path", None, None), P(), P(), P(("grp", "path"), None), P(), P())
    out_specs = (P("grp", "state", "path", None, None), P("grp", "state", "path", None, None))
    return jax.shard_map(body, mesh=mesh, in_specs=in_specs, out_specs=out_specs, check_vma=False)
```

```python
import functools
import math

import jax
import jax.numpy as jnp
from jax import lax
from jax.experimental import pallas as pl
from jax.experimental.pallas import tpu as pltpu
from jax.sharding import PartitionSpec as P


MESH = pl.DeviceIdType.MESH


def window_kernel(
    n,
    pairs,
    scale,
    half_block,
    base_ref,
    ext_ref,
    first_ref,
    top_ref,
    kept_ref,
    arrived_ref,
    vals_ref,
    held_ref,
    exts_ref,
    middle_ref,
    stack_ref,
    packed_ref,
    turned_ref,
    final_ref,
    vals_buf,
    own_sem,
    send_sem,
    recv_sem,
    ext_send,
    ext_recv,
    vals_sem,
    kept_sem,
    swap_sem,
):
    g, k, c = lax.axis_index("grp"), lax.axis_index("path"), lax.axis_index("state")
    dimension = base_ref.shape[1]
    variants = top_ref.shape[0]
    selected = top_ref.shape[1] - 2 * half_block
    odd = lax.rem(k, 2)
    pos = (1 - odd) * (k // 2) + odd * (n - 1 - k // 2)

    def place(p):
        p = lax.rem(p + n, n)
        high = p // (n // 2)
        return (1 - high) * (2 * p) + high * (2 * (n - 1 - p) + 1)

    right, left = (g, place(pos + 1), c), (g, place(pos - 1), c)
    side = lax.rem(g, 2) if pairs else 0
    partner = (g + 1 - 2 * side, k, c)
    twin = (g, k, 1 - c)

    barrier = pltpu.get_barrier_semaphore()
    greeted = [(g, lax.rem(k + d, n), c) for d in range(1, n)] + [twin]
    if pairs:
        greeted.append(partner)
    for other in greeted:
        pl.semaphore_signal(barrier, inc=1, device_id=other, device_id_type=MESH)
    pl.semaphore_wait(barrier, len(greeted))

    outer = (dimension + 2) // 3 if pairs else dimension // 2
    middle = dimension - 2 * outer if pairs else dimension - outer

    def cut(start, length):
        half = (length + 1) // 2
        return ((start, half), (start + half, length - half))

    far = dimension - outer
    runs = (
        cut(side * far if pairs else 0, outer),
        cut(outer, middle),
        cut((1 - side) * far if pairs else 0, outer),
    )

    started = []

    def start(item):
        item.start()
        started.append(item)

    def remote(source, target_ref, send, recv, device):
        return pltpu.make_async_remote_copy(
            src_ref=source,
            dst_ref=target_ref,
            send_sem=send,
            recv_sem=recv,
            device_id=device,
            device_id_type=MESH,
        )

    def on_ring(stream, u, step, piece, block, source, target):
        first, length = runs[stream][piece]
        ref = held_ref.at[block, u, pl.ds(first, length)]
        if source is not None:
            source = source.at[u, pl.ds(first, length)]
        index = (stream, u, step - 1, piece)
        return remote(
            ref if source is None else source, ref, send_sem.at[index], recv_sem.at[index], target
        )

    def arriving(stream, u, step, piece):
        block = place(pos + step) if stream == 1 else place(pos - step)
        return on_ring(stream, u, step, piece, block, None, left)

    work = []

    def advance(u, step):
        for piece in range(2):
            if work:
                work.pop(0)()
            for stream, target in ((0, right), (1, left)):
                if step > 0:
                    arriving(stream, u, step, piece).wait_recv()
                block = place(pos + step) if stream == 1 else place(pos - step)
                if step < n - 1:
                    source = base_ref if step == 0 else None
                    start(on_ring(stream, u, step + 1, piece, block, source, target))
                if pairs and stream == 0 and step > 0:
                    first, length = runs[0][piece]
                    ref = held_ref.at[block, u, pl.ds(first, length)]
                    index = (2, u, step - 1, piece)
                    start(remote(ref, ref, send_sem.at[index], recv_sem.at[index], partner))

    def settle(u):
        if pairs:
            for step in range(1, n):
                for piece in range(2):
                    arriving(2, u, step, piece).wait_recv()

    def choose():
        for d in range(1, n):
            block = exts_ref.at[lax.rem(k - d + n, n)]
            remote(block, block, ext_send.at[d - 1], ext_recv.at[d - 1], twin).wait_recv()
        codes = []
        for section in range(2):
            total = exts_ref[0, selected + section].astype(jnp.float32)
            for d in range(1, n):
                total = total + exts_ref[d, selected + section].astype(jnp.float32)
            codes.append(total)
        def select(p):
            hits = [
                [jnp.where(code[p : p + 1] == float(v), 1.0, 0.0) for v in range(variants)]
                for code in codes
            ]
            total = first_ref[0, :dimension] * hits[0][0]
            for v in range(1, variants):
                total = total + first_ref[v, :dimension] * hits[0][v]
            middle_ref[p] = total.astype(jnp.bfloat16)
            for part in range(2):
                span = slice(part * half_block, (part + 1) * half_block)
                total = top_ref[0, span] * hits[1][0]
                for v in range(1, variants):
                    total = total + top_ref[v, span] * hits[1][v]
                stack_ref[pl.ds((part * n + p) * half_block, half_block), :] = total

        def values():
            packed_ref[...] = stack_ref[...].astype(jnp.bfloat16)
            lanes = lax.broadcasted_iota(jnp.int32, (n, dimension), 1)
            out = jnp.zeros((n, dimension), jnp.float32)
            for j in range(selected):
                rows, weights = [], []
                for picked, at, code, into in (
                    (top_ref, 2 * half_block + j, codes[1], rows),
                    (first_ref, dimension + j, codes[0], weights),
                ):
                    total = jnp.zeros((n, dimension), jnp.float32)
                    for v in range(variants):
                        hit = jnp.where(code[:n] == float(v), 1.0, 0.0)
                        total = total + hit * picked[v, at : at + 1, :]
                    into.append(total)
                columns = exts_ref[:, j].reshape(dimension, dimension)
                mixed = jnp.dot(
                    rows[0].astype(jnp.bfloat16), columns, preferred_element_type=jnp.float32
                )
                value = jnp.sum(mixed * weights[0], axis=1, keepdims=True)
                out = jnp.where(lanes == j, value, out)
            vals_buf[0] = out.astype(jnp.bfloat16).astype(jnp.float32) * scale

        return [functools.partial(select, p) for p in range(n)] + [values]

    def mix_top(u, low, high):
        def one(i, carry):
            blocks = [held_ref[:, u, 2 * i + e].reshape(dimension, dimension) for e in range(2)]
            mixed = jnp.dot(
                packed_ref[...],
                jnp.concatenate(blocks, axis=1),
                preferred_element_type=jnp.float32,
            )
            for e in range(2):
                turned_ref[pl.ds(2 * i + e, dimension, stride=dimension), :] = mixed[
                    :, e * dimension : (e + 1) * dimension
                ]
            return carry

        lax.fori_loop(low // 2, high // 2, one, 0, unroll=2)

    def mix_middle(u, low, high):
        def one(p, carry):
            matrix = middle_ref[p]
            for part in range(2):
                for w in range(0, half_block, 2):
                    row = (part * n + p) * half_block + w
                    begin = pl.multiple_of(row * dimension, dimension)
                    blocks = [
                        turned_ref[pl.ds(begin + e * dimension, dimension), :].astype(jnp.bfloat16)
                        for e in range(2)
                    ]
                    mixed = jnp.dot(
                        matrix,
                        jnp.concatenate(blocks, axis=1),
                        preferred_element_type=jnp.float32,
                    ).astype(jnp.bfloat16)
                    for e in range(2):
                        final_ref[u, part, p, w + e] = mixed[:, e * dimension : (e + 1) * dimension]
            return carry

        lax.fori_loop(low, high, one, 0)

    kept = []
    quarter = n // 4

    def release(u, q):
        span = pl.ds(q * quarter, quarter)
        start(
            remote(
                final_ref.at[u, 1, span],
                arrived_ref.at[u, span],
                swap_sem.at[0, u, q],
                swap_sem.at[1, u, q],
                twin,
            )
        )
        item = pltpu.make_async_copy(
            final_ref.at[u, 0, span], kept_ref.at[u, span], kept_sem.at[u, q]
        )
        item.start()
        kept.append(item)

    for d in range(1, n):
        start(
            remote(
                ext_ref,
                exts_ref.at[k],
                ext_send.at[d - 1],
                ext_recv.at[d - 1],
                (g, lax.rem(k + d, n), c),
            )
        )
    own = pltpu.make_async_copy(base_ref, held_ref.at[k], own_sem.at[0])
    own.start()
    own_ext = pltpu.make_async_copy(ext_ref, exts_ref.at[k], own_sem.at[1])
    own_ext.start()
    advance(0, 0)
    advance(0, 1)
    own_ext.wait()
    own.wait()
    work.extend(choose())
    for step in range(2, n - 1):
        advance(0, step)
    while work:
        work.pop(0)()
    advance(1, 0)
    advance(0, n - 1)
    settle(0)
    start(remote(vals_buf.at[0], vals_buf.at[1], vals_sem.at[0], vals_sem.at[1], twin))
    for q in range(8):
        work.append(functools.partial(mix_top, 0, q * dimension // 8, (q + 1) * dimension // 8))
    for q in range(n):
        work.append(functools.partial(mix_middle, 0, q, q + 1))
    for step in range(1, n):
        advance(1, step)
    while work:
        work.pop(0)()
    settle(1)
    for q in range(4):
        release(0, q)
    mix_top(1, 0, dimension)
    for q in range(4):
        mix_middle(1, q * quarter, (q + 1) * quarter)
        if q > 0:
            release(1, q - 1)
    remote(
        vals_buf.at[0], vals_buf.at[1], vals_sem.at[0], vals_sem.at[1], twin
    ).wait_recv()
    vals_ref[...] = vals_buf[...]
    release(1, 3)
    for u in range(2):
        for q in range(4):
            span = pl.ds(q * quarter, quarter)
            remote(
                final_ref.at[u, 1, span],
                arrived_ref.at[u, span],
                swap_sem.at[0, u, q],
                swap_sem.at[1, u, q],
                twin,
            ).wait_recv()
    for item in started:
        item.wait_send()
    for item in kept:
        item.wait()


def window(base, ext, first, top, half_block, n, scale):
    pairs = lax.axis_size("grp") % 2 == 0
    streams = 3 if pairs else 2
    dimension = base.shape[1]
    state = (2, n, half_block, dimension, dimension)
    vmem = pl.BlockSpec(memory_space=pltpu.VMEM)
    hbm = pl.BlockSpec(memory_space=pl.ANY)
    return pl.pallas_call(
        functools.partial(window_kernel, n, pairs, scale, half_block),
        out_shape=[
            jax.ShapeDtypeStruct(state, jnp.bfloat16),
            jax.ShapeDtypeStruct(state, jnp.bfloat16),
            jax.ShapeDtypeStruct((2, n, dimension), jnp.float32),
        ],
        in_specs=[vmem] * 4,
        out_specs=[hbm, hbm, vmem],
        scratch_shapes=[
            pltpu.VMEM((n,) + base.shape, base.dtype),
            pltpu.VMEM((n,) + ext.shape, ext.dtype),
            pltpu.VMEM((n, dimension, dimension), jnp.bfloat16),
            pltpu.VMEM((dimension, dimension), jnp.float32),
            pltpu.VMEM((dimension, dimension), jnp.bfloat16),
            pltpu.VMEM((dimension * dimension, dimension), jnp.float32),
            pltpu.VMEM((2,) + state, jnp.bfloat16),
            pltpu.VMEM((2, n, dimension), jnp.float32),
            pltpu.SemaphoreType.DMA((2,)),
            pltpu.SemaphoreType.DMA((streams, 2, n - 1, 2)),
            pltpu.SemaphoreType.DMA((streams, 2, n - 1, 2)),
            pltpu.SemaphoreType.DMA((n - 1,)),
            pltpu.SemaphoreType.DMA((n - 1,)),
            pltpu.SemaphoreType.DMA((2,)),
            pltpu.SemaphoreType.DMA((2, 4)),
            pltpu.SemaphoreType.DMA((2, 2, 4)),
        ],
        compiler_params=pltpu.CompilerParams(
            collective_id=0, has_side_effects=True, vmem_limit_bytes=52 * 2**20
        ),
    )(base, ext, first, top)


def fused_join_kernel(paths, selected, vals_ref, core_ref, kept_ref, arrived_ref, *outs):
    dimension = kept_ref.shape[-1]
    step = 32
    for core in range(2):

        @pl.when(core_ref[0] == core)
        def _(core=core):
            for source, out, base in (
                (kept_ref, outs[core], paths * dimension),
                (arrived_ref, outs[1 - core], 0),
            ):
                for u in range(2):

                    def chunk(i, carry, source=source, out=out, base=base, u=u):
                        start = pl.multiple_of(i * step, step)
                        loaded = [
                            source[u, p, 0, pl.ds(start, step), :].astype(jnp.float32)
                            for p in range(paths)
                        ]
                        for j in range(selected):
                            total = loaded[0] * vals_ref[base + j]
                            for p in range(1, paths):
                                total = total + loaded[p] * vals_ref[base + p * dimension + j]
                            out[j, 0, u, pl.ds(start, step), :] = total
                        return carry

                    lax.fori_loop(0, dimension // step, chunk, 0)


def fused_join(vals, core, kept, arrived, selected):
    _, paths, half_block, dimension, _ = kept.shape
    spec = pl.BlockSpec((2, paths, 1, dimension, dimension), lambda w, *_: (0, 0, w, 0, 0))
    out_spec = pl.BlockSpec(
        (selected, 1, 2, dimension, dimension), lambda w, *_: (0, w, 0, 0, 0)
    )
    out = jax.ShapeDtypeStruct((selected, half_block, 2, dimension, dimension), jnp.float32)
    return pl.pallas_call(
        functools.partial(fused_join_kernel, paths, selected),
        grid_spec=pltpu.PrefetchScalarGridSpec(
            num_scalar_prefetch=2,
            grid=(half_block,),
            in_specs=[spec] * 2,
            out_specs=[out_spec] * 2,
        ),
        out_shape=[out, out],
        compiler_params=pltpu.CompilerParams(vmem_limit_bytes=50 * 2**20),
    )(vals, core, kept, arrived)


def mixes(gates, cuts, bits, columns=None):
    dimension = gates.shape[-1]
    count = bits.shape[1]
    rows = lax.broadcasted_iota(jnp.int32, (dimension, dimension), 0)
    cols = lax.broadcasted_iota(jnp.int32, (dimension, dimension), 1)
    if columns is not None:
        cols = columns(cols)
    block = 2**count
    kernel = jnp.where(rows // block == cols // block, 1.0, 0.0).astype(jnp.float32)
    for k in reversed(range(count)):
        picked = jnp.where(
            (bits[:, k] == 1)[:, None, None, None], cuts[None, :, k, 1], cuts[None, :, k, 0]
        )
        low_row = rows // 2**k % 2 == 1
        low_col = cols // 2**k % 2 == 1
        entry = [[picked[:, :, a, b, None, None] for b in range(2)] for a in range(2)]
        factor = jnp.where(
            low_row,
            jnp.where(low_col, entry[1][1], entry[1][0]),
            jnp.where(low_col, entry[0][1], entry[0][0]),
        )
        kernel = kernel * factor
    return jnp.einsum(
        "hij,phjk->phik",
        gates.astype(jnp.float32),
        kernel,
        precision=lax.Precision.HIGHEST,
        preferred_element_type=jnp.float32,
    ).astype(jnp.bfloat16)


def turn_kernel(paths, half_block, states_ref, top_ref, middle_ref, out_ref, turned_ref):
    dimension = middle_ref.shape[-1]
    rows = top_ref.shape[0]

    def mix_top(y, carry):
        block = states_ref[:, 0, y].reshape(dimension, dimension)
        turned_ref[pl.ds(y, rows, stride=dimension), :] = jnp.dot(
            top_ref[...], block, preferred_element_type=jnp.float32
        )
        return carry

    lax.fori_loop(0, dimension, mix_top, 0, unroll=4)

    def mix_middle(p, carry):
        matrix = middle_ref[p]
        for side in range(2):
            for w in range(half_block):
                row = (side * paths + p) * half_block + w
                start = pl.multiple_of(row * dimension, dimension)
                block = turned_ref[pl.ds(start, dimension), :].astype(jnp.bfloat16)
                out_ref[side, p, w] = jnp.dot(
                    matrix, block, preferred_element_type=jnp.float32
                ).astype(jnp.bfloat16)
        return carry

    lax.fori_loop(0, paths, mix_middle, 0)


def turn(states, top, middle, u):
    owners, _, dimension, near, _ = states.shape
    paths = middle.shape[0]
    half_block = near // 2
    return pl.pallas_call(
        functools.partial(turn_kernel, paths, half_block),
        grid=(1,),
        in_specs=[
            pl.BlockSpec(
                (owners, 1, dimension, near, dimension),
                lambda i: (0, u, 0, 0, 0),
                pipeline_mode=pl.Buffered(1),
            ),
            pl.BlockSpec(top.shape, lambda i: (0, 0)),
            pl.BlockSpec(middle.shape, lambda i: (0, 0, 0)),
        ],
        out_specs=pl.BlockSpec(
            (2, paths, half_block, dimension, dimension), lambda i: (0, 0, 0, 0, 0)
        ),
        out_shape=jax.ShapeDtypeStruct(
            (2, paths, half_block, dimension, dimension), jnp.bfloat16
        ),
        scratch_shapes=[pltpu.VMEM((top.shape[0] * dimension, dimension), jnp.float32)],
        compiler_params=pltpu.CompilerParams(vmem_limit_bytes=50 * 2**20),
        cost_estimate=pl.CostEstimate(
            flops=4 * top.shape[0] * dimension**3,
            bytes_accessed=4 * dimension**3 * 2,
            transcendentals=0,
        ),
    )(states, top, middle)


def join_kernel(paths, selected, vals_ref, *refs):
    mine = refs[:2]
    other = refs[2:4]
    outs = refs[4:]
    c = vals_ref[2 * paths * selected]
    dimension = mine[0].shape[-1]
    step = 32

    for u in range(2):
        for source, which in ((mine[u], 0), (other[u], 1)):
            half = c if which == 0 else 1.0 - c
            for h in range(2):

                @pl.when(half == float(h))
                def _(source=source, h=h, u=u):
                    def chunk(i, carry):
                        start = pl.multiple_of(i * step, step)
                        loaded = [
                            source[p, 0, pl.ds(start, step), :].astype(jnp.float32)
                            for p in range(paths)
                        ]
                        for j in range(selected):
                            base = (1 - h) * paths * selected + j
                            total = loaded[0] * vals_ref[base]
                            for p in range(1, paths):
                                total = total + loaded[p] * vals_ref[base + p * selected]
                            outs[h][j, 0, u, pl.ds(start, step), :] = total
                        return carry

                    lax.fori_loop(0, dimension // step, chunk, 0)


def join(vals, mine, other):
    paths, half_block, dimension, _ = mine[0].shape
    selected = vals.shape[0] // (2 * paths)
    spec = pl.BlockSpec((paths, 1, dimension, dimension), lambda w, *_: (0, w, 0, 0))
    out_spec = pl.BlockSpec(
        (selected, 1, 2, dimension, dimension), lambda w, *_: (0, w, 0, 0, 0)
    )
    out = jax.ShapeDtypeStruct((selected, half_block, 2, dimension, dimension), jnp.float32)
    return pl.pallas_call(
        functools.partial(join_kernel, paths, selected),
        grid_spec=pltpu.PrefetchScalarGridSpec(
            num_scalar_prefetch=1,
            grid=(half_block,),
            in_specs=[spec] * 4,
            out_specs=[out_spec] * 2,
        ),
        out_shape=[out, out],
        compiler_params=pltpu.CompilerParams(vmem_limit_bytes=50 * 2**20),
    )(vals, *mine, *other)


def body_fused(base, block_gates, cut_ops, path_bits, own_picks):
    sections = path_bits.shape[1] // 2
    c, k, owners = lax.axis_index("state"), lax.axis_index("path"), lax.axis_size("path")
    dimension = base.shape[-1]
    near = base.shape[2]
    half_block = near // 2
    selected = own_picks.shape[0]
    variants = 2**sections
    powers = 2 ** jnp.arange(sections, dtype=jnp.int32)
    every = jnp.arange(variants, dtype=jnp.int32)[:, None] // powers[None, :] % 2

    def of_half(array):
        return lax.dynamic_index_in_dim(array, c, 0, keepdims=False)

    every_lane = jnp.arange(dimension)
    z_hot = (own_picks[:, None] % dimension == every_lane).astype(jnp.bfloat16)
    y_hot = (own_picks[:, None] // dimension % dimension == every_lane).astype(jnp.bfloat16)
    w_hot = (own_picks[:, None] // (dimension * dimension) // 2 == every_lane).astype(jnp.bfloat16)
    second, third = of_half(block_gates[1]), of_half(block_gates[2])
    ops = of_half(cut_ops)

    def picked(hot, gate):
        return jnp.dot(hot, gate, preferred_element_type=jnp.float32).astype(jnp.bfloat16)

    first = mixes(
        jnp.concatenate([second, picked(y_hot, second)])[None], ops[None, :sections], every
    )[:, 0].astype(jnp.float32)

    def columns_of(q):
        return q // half_block % 2 * (dimension // 2) + q // near * half_block + q % half_block

    rows = third.reshape(2, owners, half_block, dimension)
    rows = lax.dynamic_index_in_dim(rows, k, 1, keepdims=False)
    rows = jnp.where(c == 1, rows[::-1], rows).reshape(near, dimension)
    top = mixes(
        jnp.concatenate([rows, picked(w_hot, third)])[None], ops[None, sections:], every, columns_of
    )[:, 0].astype(jnp.float32)

    lanes = jnp.einsum("jz,uyvz->juvy", z_hot, base, preferred_element_type=jnp.float32)
    u_own = own_picks // (dimension * dimension) % 2
    columns = jnp.where(u_own[:, None, None] == 1, lanes[:, 1], lanes[:, 0]).astype(jnp.bfloat16)
    codes = jnp.sum(path_bits.reshape(2, sections) * powers[None, :], axis=1)
    spot = jnp.arange(near)[None, :, None] == k
    marks = jnp.where(spot, codes[:, None, None], 0).astype(jnp.bfloat16)
    ext = jnp.concatenate([columns, jnp.broadcast_to(marks, (2, near, dimension))], axis=0)

    kept, arrived, vals = window(
        base, ext, first, top, half_block, owners, 1.0 / math.sqrt(owners)
    )
    outs = fused_join(vals.reshape(-1), c[None].astype(jnp.int32), kept, arrived, selected)
    return tuple(out.reshape(selected, 1, near, dimension, dimension) for out in outs)


def body(start_states, block_gates, cut_ops, path_bits, left_pick, right_pick):
    sections = path_bits.shape[1] // 2
    c = lax.axis_index("state")
    k = lax.axis_index("path")
    owners = lax.axis_size("path")
    dimension = start_states.shape[-1]
    half_block = dimension // (2 * owners)
    near = 2 * half_block
    per_device = path_bits.shape[0]
    paths = owners * per_device
    selected = left_pick.shape[0]

    mine = lax.all_to_all(start_states, "state", split_axis=0, concat_axis=1, tiled=True)
    mine = mine.reshape(2, half_block, 2, dimension, dimension)
    laid = jnp.transpose(mine, (2, 3, 0, 1, 4)).reshape(2, dimension, near, dimension)
    gate = lax.dynamic_index_in_dim(block_gates[0], c, 0, keepdims=False)
    base = jnp.einsum(
        "uyvz,iz->uyvi", laid, gate, preferred_element_type=jnp.float32
    ).astype(jnp.bfloat16)

    picks = jnp.stack([left_pick, right_pick])
    own_picks = lax.dynamic_index_in_dim(picks, c, 0, keepdims=False)
    if per_device == 1 and owners % 4 == 0 and owners <= 8 and near % 16 == 0:
        return body_fused(base, block_gates, cut_ops, path_bits, own_picks)

    z_hot = (own_picks[:, None] % dimension == jnp.arange(dimension)[None, :]).astype(jnp.bfloat16)
    lanes = jnp.einsum("jz,uyvz->juyv", z_hot, base, preferred_element_type=jnp.float32)
    u_own = own_picks // (dimension * dimension) % 2
    near_pick = jnp.where(u_own[:, None, None] == 1, lanes[:, 1], lanes[:, 0])
    small = jnp.concatenate(
        [
            near_pick.astype(jnp.bfloat16).reshape(-1),
            jnp.pad(path_bits.astype(jnp.bfloat16), ((0, 0), (0, dimension - 2 * sections))).reshape(-1),
        ]
    )
    pooled = lax.all_gather(small, ("path", "state"), axis=0)
    size = selected * dimension * near
    bits = pooled[:, size:].reshape(owners, 2, per_device, dimension)[:, 0, :, : 2 * sections]
    bits = bits.reshape(paths, 2 * sections).astype(jnp.int32)
    columns = pooled[:, :size].reshape(owners, 2, selected, dimension, near)

    gathered = lax.all_gather(base, "path", axis=0)

    mix1 = mixes(block_gates[1], cut_ops[:, :sections], bits[:, :sections])
    mix2 = mixes(block_gates[2], cut_ops[:, sections:], bits[:, sections:])
    turned2 = jnp.transpose(
        mix2.reshape(paths, 2, dimension, 2, owners, half_block), (0, 1, 2, 4, 3, 5)
    ).reshape(paths, 2, dimension, dimension)

    row_y = picks // dimension % dimension
    row_w = picks // (dimension * dimension) // 2
    y_hot = (row_y[:, :, None] == jnp.arange(dimension)).astype(jnp.bfloat16)
    w_hot = (row_w[:, :, None] == jnp.arange(dimension)).astype(jnp.bfloat16)
    m1_rows = jnp.einsum("hjy,phyk->phjk", y_hot, mix1, preferred_element_type=jnp.float32)
    m2_rows = jnp.einsum("hjw,phwv->phjv", w_hot, turned2, preferred_element_type=jnp.float32)
    cols = jnp.transpose(columns, (1, 2, 3, 0, 4)).reshape(2, selected, dimension, dimension)
    first = jnp.einsum(
        "phjy,hjyv->phjv",
        m1_rows.astype(jnp.bfloat16),
        cols,
        preferred_element_type=jnp.float32,
    ).astype(jnp.bfloat16)
    vals = jnp.sum(first.astype(jnp.float32) * m2_rows, axis=-1).astype(jnp.bfloat16)
    scale = 1.0 / math.sqrt(paths)
    flat = jnp.transpose(vals.astype(jnp.float32) * scale, (1, 0, 2)).reshape(-1)
    flat = jnp.concatenate([flat, c.astype(jnp.float32)[None]])

    own2 = lax.dynamic_index_in_dim(turned2, c, 1, keepdims=False)
    own2 = own2.reshape(paths, 2, owners, half_block, dimension)
    own2 = lax.dynamic_index_in_dim(own2, k, 2, keepdims=False)
    own2 = jnp.where(c == 1, own2[:, ::-1], own2)
    top = jnp.transpose(own2, (1, 0, 2, 3)).reshape(2 * paths * half_block, dimension)
    middle = lax.dynamic_index_in_dim(mix1, c, 1, keepdims=False)

    kept, arrived = [], []
    for u in range(2):
        both = turn(gathered, top, middle, u)
        kept.append(both[0])
        arrived.append(lax.ppermute(both[1], "state", [(0, 1), (1, 0)]))
    outs = join(flat, kept, arrived)
    return tuple(out.reshape(selected, 1, near, dimension, dimension) for out in outs)


def solution(mesh):
    in_specs = (P(None, "state", "path", None, None), P(), P(), P(("grp", "path"), None), P(), P())
    out_specs = (P("grp", "state", "path", None, None), P("grp", "state", "path", None, None))
    return jax.shard_map(body, mesh=mesh, in_specs=in_specs, out_specs=out_specs, check_vma=False)
```
